32 devices in a mesh: dp: 4 (over x, core), seq: 8 (over z, y).
Axes of the slice: x: 2, y: 2, z: 4, core: 2. Of those that a mesh axis runs over, the one named last changes fastest.
Arguments:
- block_input: bfloat16 [4, 1024, 1024], P('dp', 'seq'), may hold values from -6 to 6
- segment_ids: int32 [4, 1024], P('dp', 'seq'), may hold values from 0 to 3, never falling along the last dimension, each value on 1 to 512 neighbouring positions
- norm_gain: bfloat16 [1024], P(('dp', 'seq')), may hold values from 0.5 to 1.5
- w_qkv: bfloat16 [1024, 4096], P(None, ('dp', 'seq')), may hold values from -0.1875 to 0.1875
- w_ab: bfloat16 [1024, 16], P(('dp', 'seq')), may hold values from -0.1875 to 0.1875
- w_og: bfloat16 [1024, 2048], P(None, ('dp', 'seq')), may hold values from -0.1875 to 0.1875
- conv_w: bfloat16 [4, 4096], P(None, ('dp', 'seq')), may hold values from -3 to 3
- a_log: float32 [8], replicated, may hold values from -8 to -2
- dt_bias: float32 [8], replicated, may hold values from -2 to 1
- o_gain: float32 [256], replicated, may hold values from 0.5 to 1.5
- w_o: bfloat16 [2048, 1024], P(('dp', 'seq')), may hold values from -0.125 to 0.125
- mlp_gain: bfloat16 [1024], P(('dp', 'seq')), may hold values from 0.5 to 1.5
- w_gu: bfloat16 [1024, 5632], P('seq', 'dp'), may hold values from -0.1875 to 0.1875
- w_down: bfloat16 [2816, 1024], P('dp', 'seq'), may hold values from -0.109375 to 0.109375
- cotangent: bfloat16 [4, 1024, 1024], P('dp', 'seq'), may hold values from -6 to 6
Outputs:
- block_output: bfloat16 [4, 1024, 1024], P('dp', 'seq')
- d_x: bfloat16 [4, 1024, 1024], P('dp', 'seq')
- d_norm_gain: float32 [1024], P(('dp', 'seq'))
- d_w_qkv: float32 [1024, 4096], P(None, ('dp', 'seq'))
- d_w_ab: float32 [1024, 16], P(('dp', 'seq'))
- d_w_og: float32 [1024, 2048], P(None, ('dp', 'seq'))
- d_conv_w: float32 [4, 4096], P(None, ('dp', 'seq'))
- d_a_log: float32 [8], replicated
- d_dt_bias: float32 [8], replicated
- d_o_gain: float32 [256], replicated
- d_w_o: float32 [2048, 1024], P(('dp', 'seq'))
- d_mlp_gain: float32 [1024], P(('dp', 'seq'))
- d_w_gu: float32 [1024, 5632], P('seq', 'dp')
- d_w_down: float32 [2816, 1024], P('dp', 'seq')
The draws below stay inside these ranges and needn't reach their ends.
Inputs may be any that keep to these rules, and one draw needn't show every extreme that they name: `segment_ids`: within each sequence the ids start at 0, never fall and name 4 segments; each segment holds at most 512 tokens and one holds exactly that many.
All inputs are finite; a program needn't handle non-finite values.
Results may differ from the reference program's by a relative error of at most 0.018.
Values may be sent and summed in bfloat16 or wider, within the bound.
No kernel may reach another device: no remote copies, remote signals or barrier semaphores. Data moves between devices by JAX's collectives and lax.ppermute only.
A program may use at most 256 MiB of HBM per device.

```python
import math
import jax
import jax.numpy as jnp
import numpy as np
from jax import lax

D = 1024
HEADS = 8
DK = 128
DV = 256
FF = 2816
CONV = 4
GROUP = 64
SEGS = 4
LENGTH = 1024
SEQS = 4
CHANNELS = 4096


def steps_of(stream_key, dims, shards, low, largest):
    def one(position, parts):
        heights = jax.random.uniform(jax.random.fold_in(jax.random.fold_in(stream_key, 6), position), (parts,), jnp.float32, low / len(shards), largest / len(shards))
        return jnp.repeat(jnp.exp(heights), dims[position] // parts).reshape((-1,) + (1,) * (len(dims) - position - 1))

    level = one(*shards[0])
    for cut in shards[1:]:
        level = level * one(*cut)
    return level


def split_up(amount, total, bound, skew):
    portions = [(1 << 20) // math.isqrt(standing ** skew) + 1 for standing in range(2, amount + 1)]
    surplus, counts = total - bound - (amount - 1), [1] * (amount - 1)
    while surplus > 0:
        candidates = [i for i in range(amount - 1) if counts[i] < bound]
        mass, budget = sum([portions[i] for i in candidates]), surplus
        for i in candidates:
            addition = min(bound - counts[i], max(1, budget * portions[i] // mass), surplus)
            counts[i] = counts[i] + addition
            surplus = surplus - addition
    return np.array([bound] + counts)


def ragged_sizes(stream_key, count, total, most, skew):
    if count == 2:
        one = jax.random.randint(stream_key, (), max(1, total - most), min(most, total - 1) + 1)
        return jnp.stack([one, total - one])
    tallies = jnp.asarray(split_up(count, total, most, skew), jnp.int32)
    couples = (count - 1) // 2
    donor, sink = tallies[1:1 + 2 * couples:2], tallies[2:2 + 2 * couples:2]
    room = jnp.minimum(donor - 1, most - sink)
    passed = jax.random.randint(jax.random.fold_in(stream_key, 1), (couples,), 0, 1 << 20) % (room + 1)
    tallies = tallies.at[1:1 + 2 * couples:2].set(donor - passed).at[2:2 + 2 * couples:2].set(sink + passed)
    return tallies[jax.random.permutation(jax.random.fold_in(stream_key, 2), count)]


def centred(stream_key, extent, scale, reach, pieces=(), kind=jnp.bfloat16):
    values = jax.random.normal(stream_key, extent, jnp.float32) * scale
    if len(pieces) > 0:
        values = steps_of(stream_key, extent, pieces, -0.22, 0.18) * values
    return jnp.clip(values, min=-reach, max=reach).astype(kind)


def setup_inputs(seed: int = 0) -> dict:
    key_list = jax.random.split(jax.random.key(seed), 16)
    block_input = centred(key_list[0], (SEQS, LENGTH, D), 1.0, 6.0, ((0, 4), (1, 8)))
    segment_ids = jax.vmap(lambda own: jnp.searchsorted(jnp.cumsum(ragged_sizes(own, SEGS, LENGTH, LENGTH // 2, 0)), jnp.arange(LENGTH), side="right"))(jax.random.split(key_list[1], SEQS)).reshape((SEQS, LENGTH)).astype(jnp.int32)
    norm_gain = jnp.clip(1.0 + 0.1 * jax.random.normal(key_list[2], (D,), jnp.float32), 0.5, 1.5).astype(jnp.bfloat16)
    w_qkv = centred(key_list[3], (D, CHANNELS), D ** -0.5, 0.1875, ((1, 32),))
    w_ab = centred(key_list[4], (D, 2 * HEADS), D ** -0.5, 0.1875, ((0, 32),))
    w_og = centred(key_list[5], (D, HEADS * DV), D ** -0.5, 0.1875, ((1, 32),))
    conv_w = centred(key_list[6], (CONV, CHANNELS), 0.5, 3.0, ((1, 32),))
    a_log = jnp.clip(jax.random.uniform(key_list[7], (HEADS,), jnp.float32, -8.0, -2.0), -8.0, -2.0)
    dt_bias = jnp.clip(jax.random.uniform(key_list[8], (HEADS,), jnp.float32, -2.0, 1.0), -2.0, 1.0)
    o_gain = jnp.clip(1.0 + 0.1 * jax.random.normal(key_list[9], (DV,), jnp.float32), 0.5, 1.5)
    w_o = centred(key_list[10], (HEADS * DV, D), (HEADS * DV) ** -0.5, 0.125, ((0, 32),))
    mlp_gain = jnp.clip(1.0 + 0.1 * jax.random.normal(key_list[11], (D,), jnp.float32), 0.5, 1.5).astype(jnp.bfloat16)
    w_gu = centred(key_list[12], (D, 2 * FF), D ** -0.5, 0.1875, ((0, 8), (1, 4)))
    w_down = centred(key_list[13], (FF, D), FF ** -0.5, 0.109375, ((0, 4), (1, 8)))
    cotangent = centred(key_list[14], (SEQS, LENGTH, D), 1.0, 6.0, ((0, 4), (1, 8)))
    return {"block_input": block_input, "segment_ids": segment_ids, "norm_gain": norm_gain, "w_qkv": w_qkv, "w_ab": w_ab, "w_og": w_og, "conv_w": conv_w, "a_log": a_log, "dt_bias": dt_bias, "o_gain": o_gain, "w_o": w_o, "mlp_gain": mlp_gain, "w_gu": w_gu, "w_down": w_down, "cotangent": cotangent}


EPS = 1e-06
HIGH = lax.Precision.HIGHEST

def rms(values, gain):
    return values * lax.rsqrt(lax.optimization_barrier(jnp.mean(values * values, axis=-1, keepdims=True)) + EPS) * gain

def swiglu(joined):
    half = joined.shape[-1] // 2
    return jax.nn.silu(joined[:, :half]) * joined[:, half:]

def convolve(extended, weights, same):
    length = same.shape[0]
    total = jnp.zeros((length, extended.shape[1]), jnp.float32)
    for i in range(CONV):
        total = total + weights[i] * extended[i:i + length] * same[:, i:i + 1]
    return jax.nn.silu(total)

def same_mask(ext_ids, seg_ids):
    length = seg_ids.shape[0]
    return jnp.stack([ext_ids[i:i + length] == seg_ids for i in range(CONV)], axis=1).astype(jnp.float32)

def split_inputs(conv_out, proj_ab, a_log, dt_bias):
    length = conv_out.shape[0]
    width = HEADS * DK
    queries = conv_out[:, :width].reshape(length, HEADS, DK)
    keys_raw = conv_out[:, width:2 * width].reshape(length, HEADS, DK)
    values = conv_out[:, 2 * width:].reshape(length, HEADS, DV)
    queries = queries * lax.rsqrt(lax.optimization_barrier(jnp.sum(queries * queries, axis=-1, keepdims=True)) + EPS) * DK ** (-0.5)
    keys_n = keys_raw * lax.rsqrt(lax.optimization_barrier(jnp.sum(keys_raw * keys_raw, axis=-1, keepdims=True)) + EPS)
    betas = jax.nn.sigmoid(proj_ab[:, :HEADS])
    decays = -jnp.exp(a_log) * jax.nn.softplus(proj_ab[:, HEADS:] + dt_bias)
    return (queries, keys_n, values, betas, decays)

def group_terms(queries, keys_n, values, betas, decays, seg_ids, prev_id):
    size = queries.shape[0]
    gamma = jnp.cumsum(decays, axis=0)
    rows_i = lax.broadcasted_iota(jnp.int32, (size, size), 0)
    cols_j = lax.broadcasted_iota(jnp.int32, (size, size), 1)
    same = seg_ids[:, None] == seg_ids[None, :]
    incl = jnp.logical_and(same, cols_j <= rows_i)
    strict = jnp.logical_and(same, cols_j < rows_i).astype(jnp.float32)
    diff = gamma[:, None, :] - gamma[None, :, :]
    lower = jnp.where(incl[:, :, None], jnp.exp(jnp.where(incl[:, :, None], diff, 0.0)), 0.0)
    lower = jnp.transpose(lower, (2, 0, 1))
    carry_in = (seg_ids == prev_id).astype(jnp.float32)
    scaled = jnp.exp(gamma) * carry_in[:, None]
    head_q = jnp.transpose(queries, (1, 0, 2))
    head_k = jnp.transpose(keys_n, (1, 0, 2))
    head_v = jnp.transpose(values, (1, 0, 2))
    head_b = betas.T
    key_dots = jnp.einsum('hid,hjd->hij', head_k, head_k, precision=HIGH)
    system = jnp.eye(size, dtype=jnp.float32)[None] + head_b[:, :, None] * lower * strict[None] * key_dots
    new_v = jax.scipy.linalg.solve_triangular(system, head_b[:, :, None] * head_v, lower=True)
    new_k = jax.scipy.linalg.solve_triangular(system, (head_b * scaled.T)[:, :, None] * head_k, lower=True)
    scores = jnp.einsum('hid,hjd->hij', head_q, head_k, precision=HIGH) * lower
    q_tilde = head_q * scaled.T[:, :, None] - jnp.einsum('hij,hjd->hid', scores, new_k, precision=HIGH)
    o_new = jnp.einsum('hij,hjv->hiv', scores, new_v, precision=HIGH)
    tail = jnp.exp(gamma[-1][:, None] - gamma.T) * (seg_ids == seg_ids[-1]).astype(jnp.float32)[None, :]
    key_tail = head_k * tail[:, :, None]
    keep = (jnp.exp(gamma[-1]) * carry_in[-1])[:, None, None]
    m_map = keep * jnp.eye(DK, dtype=jnp.float32)[None] - jnp.einsum('hjd,hje->hde', key_tail, new_k, precision=HIGH)
    b_map = jnp.einsum('hjd,hjv->hdv', key_tail, new_v, precision=HIGH)
    return (q_tilde, o_new, m_map, b_map)

def rule_sequence(queries, keys_n, values, betas, decays, seg_ids):
    length = queries.shape[0]
    blocks = length // GROUP
    seg_blocks = seg_ids.reshape(blocks, GROUP)
    prevs = jnp.concatenate([jnp.full((1,), -1, jnp.int32), seg_blocks[:-1, -1].astype(jnp.int32)])

    def step(state, item):
        q_c, k_c, v_c, b_c, d_c, s_c, p_c = item
        q_tilde, o_new, m_map, b_map = group_terms(q_c, k_c, v_c, b_c, d_c, s_c, p_c)
        out_c = o_new + jnp.einsum('hcd,hdv->hcv', q_tilde, state, precision=HIGH)
        state = jnp.einsum('hde,hev->hdv', m_map, state, precision=HIGH) + b_map
        return (state, out_c)
    init = jnp.zeros((HEADS, DK, DV), jnp.float32)
    items = (queries.reshape(blocks, GROUP, HEADS, DK), keys_n.reshape(blocks, GROUP, HEADS, DK), values.reshape(blocks, GROUP, HEADS, DV), betas.reshape(blocks, GROUP, HEADS), decays.reshape(blocks, GROUP, HEADS), seg_blocks, prevs)
    _, outs = lax.scan(step, init, items)
    return jnp.transpose(outs, (0, 2, 1, 3)).reshape(length, HEADS, DV)

def out_gate(mixed, proj_og, o_gain):
    length = mixed.shape[0]
    return rms(mixed, o_gain).reshape(length, HEADS * DV) * jax.nn.silu(proj_og)

def mixer_full(proj_qkv, proj_ab, proj_og, conv_w, a_log, dt_bias, o_gain, seg_ids):
    extended = jnp.concatenate([jnp.zeros((CONV - 1, proj_qkv.shape[1]), jnp.float32), proj_qkv], axis=0)
    ext_ids = jnp.concatenate([jnp.full((CONV - 1,), -1, jnp.int32), seg_ids.astype(jnp.int32)])
    conv_out = convolve(extended, conv_w, same_mask(ext_ids, seg_ids))
    queries, keys_n, values, betas, decays = split_inputs(conv_out, proj_ab, a_log, dt_bias)
    mixed = rule_sequence(queries, keys_n, values, betas, decays, seg_ids)
    return out_gate(mixed, proj_og, o_gain)

def reference(block_input, segment_ids, norm_gain, w_qkv, w_ab, w_og, conv_w, a_log, dt_bias, o_gain, w_o, mlp_gain, w_gu, w_down, cotangent):
    f32 = jnp.float32
    bf16 = jnp.bfloat16
    gain_one = norm_gain.astype(f32)
    gain_two = mlp_gain.astype(f32)
    taps = conv_w.astype(f32)

    def one(totals, item):
        rows, seg_ids, cot = item
        rows_f = rows.astype(f32)
        normed_f, rms1_back = jax.vjp(rms, rows_f, gain_one)
        normed = normed_f.astype(bf16)
        proj_qkv = jnp.dot(normed, w_qkv, preferred_element_type=f32).astype(bf16)
        proj_ab = jnp.dot(normed, w_ab, preferred_element_type=f32)
        proj_og = jnp.dot(normed, w_og, preferred_element_type=f32)

        def mixer(p_qkv, p_ab, p_og, c_w, alog, dtb, ogain):
            return mixer_full(p_qkv, p_ab, p_og, c_w, alog, dtb, ogain, seg_ids)
        gated_f, mix_back = jax.vjp(mixer, proj_qkv.astype(f32), proj_ab, proj_og, taps, a_log, dt_bias, o_gain)
        gated = gated_f.astype(bf16)
        resid = rows_f + jnp.dot(gated, w_o, preferred_element_type=f32)
        normed2_f, rms2_back = jax.vjp(rms, resid, gain_two)
        normed2 = normed2_f.astype(bf16)
        joined = jnp.dot(normed2, w_gu, preferred_element_type=f32)
        act_f, act_back = jax.vjp(swiglu, joined)
        act = act_f.astype(bf16)
        out = (resid + jnp.dot(act, w_down, preferred_element_type=f32)).astype(bf16)
        cot_f = cot.astype(f32)
        grad_down = jnp.dot(act.T, cot, preferred_element_type=f32)
        d_joined, = act_back(jnp.dot(cot, w_down.T, preferred_element_type=f32))
        d_joined_b = d_joined.astype(bf16)
        grad_gu = jnp.dot(normed2.T, d_joined_b, preferred_element_type=f32)
        d_resid_n, grad_g2 = rms2_back(jnp.dot(d_joined_b, w_gu.T, preferred_element_type=f32))
        d_resid = cot_f + d_resid_n
        d_resid_b = d_resid.astype(bf16)
        grad_o = jnp.dot(gated.T, d_resid_b, preferred_element_type=f32)
        d_gated = jnp.dot(d_resid_b, w_o.T, preferred_element_type=f32)
        d_qkv, d_ab, d_og, grad_conv, grad_alog, grad_dtb, grad_ogain = mix_back(d_gated)
        d_qkv_b = d_qkv.astype(bf16)
        d_ab_b = d_ab.astype(bf16)
        d_og_b = d_og.astype(bf16)
        grad_qkv = jnp.dot(normed.T, d_qkv_b, preferred_element_type=f32)
        grad_ab = jnp.dot(normed.T, d_ab_b, preferred_element_type=f32)
        grad_og = jnp.dot(normed.T, d_og_b, preferred_element_type=f32)
        d_normed = jnp.dot(d_qkv_b, w_qkv.T, preferred_element_type=f32) + jnp.dot(d_ab_b, w_ab.T, preferred_element_type=f32) + jnp.dot(d_og_b, w_og.T, preferred_element_type=f32)
        d_rows_n, grad_g1 = rms1_back(d_normed)
        d_rows = (d_resid + d_rows_n).astype(bf16)
        terms = (grad_g1, grad_qkv, grad_ab, grad_og, grad_conv, grad_alog, grad_dtb, grad_ogain, grad_o, grad_g2, grad_gu, grad_down)
        totals = tuple((a + b for a, b in zip(totals, terms)))
        return (totals, (out, d_rows))
    shapes = (norm_gain.shape, w_qkv.shape, w_ab.shape, w_og.shape, conv_w.shape, a_log.shape, dt_bias.shape, o_gain.shape, w_o.shape, mlp_gain.shape, w_gu.shape, w_down.shape)
    init = tuple((jnp.zeros(shape, f32) for shape in shapes))
    totals, (outs, d_rows) = lax.scan(one, init, (block_input, segment_ids, cotangent))
    return (outs, d_rows, totals[0], totals[1], totals[2], totals[3], totals[4], totals[5], totals[6], totals[7], totals[8], totals[9], totals[10], totals[11])
```

```python
import functools

import jax
import jax.numpy as jnp
from jax import lax
from jax.experimental import pallas as pl
from jax.experimental.pallas import tpu as pltpu
from jax.sharding import PartitionSpec as P

HEADS = 8
DK = 128
DV = 256
CONV = 4
BLOCK = 64
EDGE = 16
EPS = 1e-06
BOTH = ("dp", "seq")


f32 = jnp.float32
bf16 = jnp.bfloat16
HIGH = lax.Precision.HIGHEST


def rms(values, gain):
    return values * lax.rsqrt(jnp.mean(values * values, axis=-1, keepdims=True) + EPS) * gain


def swiglu(gate, up):
    return jax.nn.silu(gate) * up


def convolve(extended, weights, same):
    length = same.shape[0]
    total = jnp.zeros((length, extended.shape[1]), f32)
    for i in range(CONV):
        total = total + weights[i] * extended[i : i + length] * same[:, i : i + 1]
    return jax.nn.silu(total)


def exchange(blocks, axis):
    return lax.all_to_all(blocks, axis, 0, 0)


def spread(value, axis):
    count = lax.axis_size(axis)
    return exchange(jnp.broadcast_to(value[None], (count,) + value.shape), axis)


def swap(value, axis, bit):
    count = lax.axis_size(axis)
    return lax.ppermute(value, axis, [(i, i ^ bit) for i in range(count)])


def pair_bits(axis):
    count = lax.axis_size(axis)
    bits, bit = [], 1
    while bit < count:
        bits.append(bit)
        bit *= 2
    return bits


def pair_gather(rows, axis):
    for bit in reversed(pair_bits(axis)):
        rows = jnp.concatenate([rows, swap(rows, axis, bit)], axis=0)
    return rows


def pair_scatter(rows, axis):
    for bit in pair_bits(axis):
        half = rows.shape[0] // 2
        rows = rows[:half].astype(f32) + swap(rows[half:].astype(bf16), axis, bit).astype(f32)
    return rows


def pair_offsets(axis):
    offsets = [0]
    for bit in reversed(pair_bits(axis)):
        offsets = offsets + [offset ^ bit for offset in offsets]
    return offsets


def lookup(table, index):
    return sum(entry * (index == i).astype(jnp.int32) for i, entry in enumerate(table))


def ring_order(count):
    return list(range(0, count, 2)) + list(range(count - 1, 0, -2))


def ring_pairs(count, turn):
    order = ring_order(count)
    return [(order[r], order[(r + turn) % count]) for r in range(count)]


def ring_place(axis):
    count = lax.axis_size(axis)
    order = ring_order(count)
    place = [order.index(i) for i in range(count)]
    at = lookup(place, lax.axis_index(axis))
    return lambda ahead: lookup(order, (at + ahead + count) % count)


def together(*jobs):
    results = [None] * len(jobs)
    waiting = {}
    for i, job in enumerate(jobs):
        try:
            waiting[i] = next(job)
        except StopIteration as stop:
            results[i] = stop.value
    while waiting:
        waiting = lax.optimization_barrier(waiting)
        later = {}
        for i, received in waiting.items():
            try:
                later[i] = jobs[i].send(received)
            except StopIteration as stop:
                results[i] = stop.value
        waiting = later
    return results


def pair_gather_job(rows, axis):
    for bit in reversed(pair_bits(axis)):
        (other,) = yield (swap(rows, axis, bit),)
        rows = jnp.concatenate([rows, other], axis=0)
    return rows


def pair_scatter_job(rows, axis):
    for bit in pair_bits(axis):
        half = rows.shape[0] // 2
        (other,) = yield (swap(rows[half:].astype(bf16), axis, bit),)
        rows = rows[:half].astype(f32) + other.astype(f32)
    return rows


def ring_gather_job(block, axis, rows):
    count = lax.axis_size(axis)
    source = ring_place(axis)
    whole = jnp.zeros((count * rows, block.shape[1]), block.dtype)
    tails = jnp.zeros((count, 1, block.shape[1]), block.dtype)

    def put(whole, tails, got, ahead):
        at = source(ahead)
        return (
            lax.dynamic_update_slice_in_dim(whole, got[:rows], at * rows, 0),
            jnp.where(jnp.arange(count)[:, None, None] == at, got[rows : rows + 1][None], tails),
        )

    whole, tails = put(whole, tails, block, 0)
    one = two = block
    for k in range(1, count // 2 + 1):
        both = k < count - count // 2
        one = lax.ppermute(one, axis, ring_pairs(count, 1))
        if both:
            two = lax.ppermute(two, axis, ring_pairs(count, -1))
            one, two = yield (one, two)
            whole, tails = put(whole, tails, two, k)
        else:
            (one,) = yield (one,)
        whole, tails = put(whole, tails, one, -k)
    return whole, tails[:, 0]


def relative(values, axis):
    count = lax.axis_size(axis)
    wanted = jnp.asarray(pair_offsets(axis), jnp.int32) ^ lax.axis_index(axis)
    pick = wanted[:, None] == jnp.arange(count)[None]
    pick = pick.reshape(pick.shape + (1,) * (values.ndim - 1))
    return jnp.sum(jnp.where(pick, values[None], jnp.zeros((), values.dtype)), axis=1)


def absolute(values, axis):
    count = lax.axis_size(axis)
    wanted = jnp.asarray(pair_offsets(axis), jnp.int32) ^ lax.axis_index(axis)
    pick = jnp.arange(count)[:, None] == wanted[None]
    pick = pick.reshape(pick.shape + (1,) * (values.ndim - 1))
    return jnp.sum(jnp.where(pick, values[None], jnp.zeros((), values.dtype)), axis=1)


def ring_scatter_job(parts, axis):
    count = lax.axis_size(axis)
    source = ring_place(axis)
    part = lambda ahead: lax.dynamic_index_in_dim(parts, source(ahead), 0, keepdims=False)
    far = count // 2
    near = count - 1 - far
    one, two = part(far).astype(bf16), part(-near).astype(bf16)
    for k in range(far):
        one = lax.ppermute(one, axis, ring_pairs(count, 1))
        if k < near:
            two = lax.ppermute(two, axis, ring_pairs(count, -1))
        one, two = yield (one, two)
        if k < far - 1:
            one = (one.astype(f32) + part(far - k - 1)).astype(bf16)
        if k < near - 1:
            two = (two.astype(f32) + part(-(near - k - 1))).astype(bf16)
    return part(0) + one.astype(f32) + two.astype(f32)


def split_dot(a, b):
    a_hi, b_hi = a.astype(bf16), b.astype(bf16)
    a_lo = (a - a_hi.astype(f32)).astype(bf16)
    b_lo = (b - b_hi.astype(f32)).astype(bf16)
    dot = functools.partial(jnp.dot, preferred_element_type=f32)
    return dot(a_hi, b_hi) + (dot(a_hi, b_lo) + dot(a_lo, b_hi))


def chain_forward(m_ref, b_ref, s_ref):
    blocks, _, width = b_ref.shape

    def step(c, state):
        s_ref[c] = state
        return split_dot(m_ref[c], state) + b_ref[c]

    lax.fori_loop(0, blocks, step, jnp.zeros((DK, width), f32))


def chain_backward(mt_ref, d_ref, g_ref):
    blocks, _, width = d_ref.shape

    def step(i, grad):
        c = blocks - 1 - i
        g_ref[c] = grad
        return split_dot(mt_ref[c], grad) + d_ref[c]

    lax.fori_loop(0, blocks, step, jnp.zeros((DK, width), f32))


def run_chain(kernel, maps, terms):
    width = terms.shape[2]
    terms = jnp.pad(terms, ((0, 0), (0, 0), (0, -width % 128)))
    return pl.pallas_call(
        kernel,
        out_shape=jax.ShapeDtypeStruct(terms.shape, f32),
        in_specs=[pl.BlockSpec(memory_space=pltpu.VMEM)] * 2,
        out_specs=pl.BlockSpec(memory_space=pltpu.VMEM),
    )(maps, terms)[:, :, :width]


@jax.custom_vjp
def chain(maps, terms):
    return run_chain(chain_forward, maps, terms)


def chain_fwd(maps, terms):
    states = run_chain(chain_forward, maps, terms)
    return states, (maps, states)


def chain_bwd(saved, d_states):
    maps, states = saved
    grads = run_chain(chain_backward, jnp.swapaxes(maps, 1, 2), d_states)
    return jnp.einsum("ndv,nev->nde", grads, states, preferred_element_type=f32), grads


chain.defvjp(chain_fwd, chain_bwd)


def bdot(a, b, precision=None):
    return jnp.einsum("nij,njk->nik", a, b, precision=precision, preferred_element_type=f32)


def inverse_of(strict_lower):
    size = strict_lower.shape[-1]
    rows_i = lax.broadcasted_iota(jnp.int32, (size, size), 0)
    cols_j = lax.broadcasted_iota(jnp.int32, (size, size), 1)
    inverse = jnp.broadcast_to(jnp.eye(size, dtype=f32), strict_lower.shape)
    width = 1
    while width < size:
        inside = (rows_i // (2 * width) == cols_j // (2 * width)) & (
            rows_i // width != cols_j // width
        )
        part = jnp.where(inside, strict_lower, 0.0)
        if width == 1:
            inverse = inverse - part
        else:
            inverse = inverse - bdot(bdot(inverse, part, HIGH), inverse, HIGH)
        width *= 2
    return inverse


@jax.custom_vjp
def unit_inverse(strict_lower):
    return inverse_of(strict_lower)


def unit_inverse_fwd(strict_lower):
    inverse = inverse_of(strict_lower)
    return inverse, inverse


def unit_inverse_bwd(inverse, d_inverse):
    flipped = jnp.swapaxes(inverse, 1, 2)
    return (-bdot(bdot(flipped, d_inverse, HIGH), flipped, HIGH),)


unit_inverse.defvjp(unit_inverse_fwd, unit_inverse_bwd)


def head_rule(queries, keys, values, betas, decays, seg_ids):
    length = queries.shape[0]
    size = min(BLOCK, length)
    blocks = length // size
    q = queries.reshape(blocks, size, DK)
    k = keys.reshape(blocks, size, DK)
    v = values.reshape(blocks, size, -1)
    beta = betas.reshape(blocks, size)
    seg = seg_ids.reshape(blocks, size)
    prev = jnp.concatenate([jnp.full((1,), -1, seg.dtype), seg[:-1, -1]])
    rows_i = lax.broadcasted_iota(jnp.int32, (size, size), 0)
    cols_j = lax.broadcasted_iota(jnp.int32, (size, size), 1)
    upto = (rows_i <= cols_j).astype(f32)
    gamma = jnp.dot(decays.reshape(blocks, size), upto, precision=HIGH)
    same = seg[:, :, None] == seg[:, None, :]
    incl = jnp.logical_and(same, (cols_j <= rows_i)[None])
    strict = jnp.logical_and(same, (cols_j < rows_i)[None]).astype(f32)
    diff = gamma[:, :, None] - gamma[:, None, :]
    lower = jnp.where(incl, jnp.exp(jnp.where(incl, diff, 0.0)), 0.0)
    carry_in = (seg == prev[:, None]).astype(f32)
    scaled = jnp.exp(gamma) * carry_in
    key_dots = jnp.einsum("nid,njd->nij", k, k, precision=HIGH)
    inverse = unit_inverse(beta[:, :, None] * lower * strict * key_dots)
    sides = jnp.concatenate([beta[:, :, None] * v, (beta * scaled)[:, :, None] * k], axis=2)
    fresh = bdot(inverse, sides, HIGH)
    new_v, new_k = fresh[:, :, : v.shape[2]], fresh[:, :, v.shape[2] :]
    scores = jnp.einsum("nid,njd->nij", q, k) * lower
    q_tilde = q * scaled[:, :, None] - bdot(scores, new_k)
    o_new = bdot(scores, new_v)
    tail = jnp.exp(gamma[:, -1:] - gamma) * (seg == seg[:, -1:]).astype(f32)
    key_tail = k * tail[:, :, None]
    keep = (jnp.exp(gamma[:, -1]) * carry_in[:, -1])[:, None, None]
    m_map = keep * jnp.eye(DK, dtype=f32)[None] - jnp.einsum("njd,nje->nde", key_tail, new_k)
    b_map = jnp.einsum("njd,njv->ndv", key_tail, new_v)
    states = chain(m_map, b_map)
    return (o_new + bdot(q_tilde, states)).reshape(length, -1)


def unit_core(proj, taps, proj_ab, a_log, dt_bias, same, seg_ids):
    extended = jnp.concatenate([jnp.zeros((CONV - 1, proj.shape[1]), f32), proj], axis=0)
    conv_out = convolve(extended, taps, same)
    queries = conv_out[:, :DK]
    keys = conv_out[:, DK : 2 * DK]
    values = conv_out[:, 2 * DK :]
    queries = (
        queries * lax.rsqrt(jnp.sum(queries * queries, axis=-1, keepdims=True) + EPS) * DK ** (-0.5)
    )
    keys = keys * lax.rsqrt(jnp.sum(keys * keys, axis=-1, keepdims=True) + EPS)
    betas = jax.nn.sigmoid(proj_ab[:, 0])
    decays = -jnp.exp(a_log) * jax.nn.softplus(proj_ab[:, 1] + dt_bias)
    return head_rule(queries, keys, values, betas, decays, seg_ids)


def out_gate(mixed, proj_og, gain, groups):
    squares = jnp.sum(mixed * mixed, axis=-1, keepdims=True)
    if groups is not None:
        squares = lax.psum(squares, "seq", axis_index_groups=groups)
    return mixed * lax.rsqrt(squares / DV + EPS) * gain * jax.nn.silu(proj_og)


class Heads:
    def __init__(self, w_qkv, w_og):
        self.ndp = lax.axis_size("dp")
        self.nseq = lax.axis_size("seq")
        self.split = self.nseq // HEADS
        self.wide = DV // self.split
        unit = lax.axis_index("seq")
        self.head = unit // self.split
        self.part = unit % self.split
        self.cq = w_qkv.shape[1]
        self.co = w_og.shape[1]
        self.direct = (
            self.split == 1
            and DK % self.cq == 0
            and (2 * DK + DV) == self.ndp * self.cq
            and DV == self.ndp * self.co
            and 2 * self.co == self.cq
        )
        if self.direct:
            per = DK // self.cq
            self.to_qkv, self.to_og = [], []
            for j in range(self.ndp * self.nseq):
                kind, head, place = 0, j // per, j % per
                if head >= HEADS:
                    kind, head = 1, head - HEADS
                if head >= HEADS:
                    own = j - 2 * HEADS * per
                    kind, head, place = 2, own // (DV // self.cq), own % (DV // self.cq)
                slot = kind * per + place
                self.to_qkv.append((j, slot * self.nseq + head))
                self.to_og.append((j, (j % self.ndp) * self.nseq + j // self.ndp))

    def back(self, pairs):
        return [(b, a) for a, b in pairs]

    def starts(self):
        base = 2 * HEADS * DK
        return (
            (self.head * DK, DK),
            ((HEADS + self.head) * DK, DK),
            (base + self.head * DV + self.part * self.wide, self.wide),
        )

    def fetch(self, w_qkv, conv_w, w_og):
        if not self.direct:
            full = lax.all_gather(w_qkv, BOTH, axis=1, tiled=True)
            taps = lax.all_gather(conv_w, BOTH, axis=1, tiled=True)
            gates = lax.all_gather(w_og, BOTH, axis=1, tiled=True)
            take = lambda a: jnp.concatenate(
                [lax.dynamic_slice_in_dim(a, s, n, 1) for s, n in self.starts()], axis=1
            )
            og = lax.dynamic_slice_in_dim(
                gates, self.head * DV + self.part * self.wide, self.wide, 1
            )
            return take(full), take(taps), og
        depth = w_qkv.shape[0]
        half = depth // 2
        padded = jnp.pad(conv_w, ((0, EDGE - CONV), (0, 0)))
        one = lax.ppermute(jnp.concatenate([w_qkv, padded], axis=0), BOTH, self.to_qkv)
        two = lax.ppermute(
            jnp.concatenate([w_og[:half], w_og[half:]], axis=1), BOTH, self.to_og
        )
        one, two = yield (one, two)
        mine = jnp.concatenate([one, two], axis=0)
        offsets = pair_offsets("dp")
        relative = yield from pair_gather_job(mine, "dp")
        relative = relative.reshape((self.ndp,) + mine.shape)
        places = [offsets.index(i) for i in range(self.ndp)]
        here = lax.axis_index("dp")
        all_slots = jnp.stack(
            [
                lax.dynamic_index_in_dim(relative, lookup(places, here ^ s), 0, keepdims=False)
                for s in range(self.ndp)
            ]
        )
        qkv = jnp.concatenate([all_slots[s, :depth] for s in range(self.ndp)], axis=1)
        taps = jnp.concatenate(
            [all_slots[s, depth : depth + CONV] for s in range(self.ndp)], axis=1
        )
        low = all_slots[:, depth + EDGE :]
        og = jnp.concatenate(
            [
                jnp.concatenate([low[s, :, : self.co], low[s, :, self.co :]], axis=0)
                for s in range(self.ndp)
            ],
            axis=1,
        )
        return qkv, taps, og

    def give(self, d_qkv, d_taps, d_og):
        depth = d_qkv.shape[0]
        half = depth // 2
        if not self.direct:
            outs = []
            for grad, total in ((d_qkv, 2 * HEADS * DK + HEADS * DV), (d_taps, None)):
                total = 2 * HEADS * DK + HEADS * DV
                full = jnp.zeros((grad.shape[0], total), f32)
                at = 0
                for start, n in self.starts():
                    full = lax.dynamic_update_slice_in_dim(
                        full, grad[:, at : at + n].astype(f32), start, 1
                    )
                    at += n
                outs.append(
                    lax.psum_scatter(full.astype(bf16), BOTH, scatter_dimension=1, tiled=True)
                )
            full = lax.dynamic_update_slice_in_dim(
                jnp.zeros((depth, HEADS * DV), f32),
                d_og.astype(f32),
                self.head * DV + self.part * self.wide,
                1,
            )
            og = lax.psum_scatter(full.astype(bf16), BOTH, scatter_dimension=1, tiled=True)
            return outs[0].astype(f32), outs[1].astype(f32), og.astype(f32)
        cq, co = self.cq, self.co
        taps = jnp.pad(d_taps.astype(bf16), ((0, EDGE - CONV), (0, 0)))
        blocks = jnp.stack(
            [
                jnp.concatenate(
                    [
                        d_qkv[:, s * cq : (s + 1) * cq],
                        taps[:, s * cq : (s + 1) * cq],
                        jnp.concatenate(
                            [
                                d_og[:half, s * co : (s + 1) * co],
                                d_og[half:, s * co : (s + 1) * co],
                            ],
                            axis=1,
                        ),
                    ],
                    axis=0,
                )
                for s in range(self.ndp)
            ]
        )
        here = lax.axis_index("dp")
        blocks = jnp.concatenate(
            [
                lax.dynamic_index_in_dim(blocks, here ^ offset, 0, keepdims=False)
                for offset in pair_offsets("dp")
            ],
            axis=0,
        )
        yield ()
        summed = (yield from pair_scatter_job(blocks, "dp")).astype(bf16)
        one = lax.ppermute(summed[: depth + EDGE], BOTH, self.back(self.to_qkv))
        two = lax.ppermute(summed[depth + EDGE :], BOTH, self.back(self.to_og))
        one, two = yield (one, two)
        one, two = one.astype(f32), two.astype(f32)
        return (
            one[:depth],
            one[depth : depth + CONV],
            jnp.concatenate([two[:, :co], two[:, co:]], axis=0),
        )


def halves_rounds(count):
    first, second = [], []
    for p in range(count):
        low = p < count // 2
        base = 2 * (p if low else p - count // 2)
        first.append((p, base if low else base + 1))
        second.append((p, base + 1 if low else base))
    return first, second


def local(
    block_input,
    segment_ids,
    norm_gain,
    w_qkv,
    w_ab,
    w_og,
    conv_w,
    a_log,
    dt_bias,
    o_gain,
    w_o,
    mlp_gain,
    w_gu,
    w_down,
    cotangent,
):
    heads = Heads(w_qkv, w_og)
    ndp, nseq, split, wide = heads.ndp, heads.nseq, heads.split, heads.wide
    rows = block_input[0]
    cot = cotangent[0]
    length, depth = rows.shape
    total = length * nseq
    small = norm_gain.shape[0]
    groups = None
    if split > 1:
        groups = [[h * split + i for i in range(split)] for h in range(HEADS)]

    full_o = lax.all_gather(w_o, BOTH, axis=0, tiled=True)
    half = w_gu.shape[1] // 2
    round_one, round_two = halves_rounds(ndp)
    low_half = lax.axis_index("dp") < ndp // 2
    even = lax.axis_index("dp") % 2 == 0

    def input_job():
        extra = jnp.concatenate(
            [norm_gain, mlp_gain, w_ab.reshape(-1), segment_ids[0].astype(bf16)]
        )
        used = extra.shape[0]
        extra = jnp.pad(extra, (0, EDGE * depth - used)).reshape(EDGE, depth)
        whole, tails = yield from ring_gather_job(
            jnp.concatenate([rows, extra], axis=0), "seq", length
        )
        params = yield from pair_gather_job(tails[None, :, : used - length], "dp")
        return whole, tails[:, used - length : used], absolute(params, "dp")

    def ffn_job():
        one = lax.ppermute(jnp.where(low_half, w_gu[:, :half], w_gu[:, half:]), "dp", round_one)
        two = lax.ppermute(jnp.where(low_half, w_gu[:, half:], w_gu[:, :half]), "dp", round_two)
        return (yield (one, two))

    (x_all, seg_ids, params), (unit_qkv, unit_taps, unit_og), (got_one, got_two) = together(
        input_job(), heads.fetch(w_qkv, conv_w, w_og), ffn_job()
    )
    seg_ids = seg_ids.astype(jnp.int32).reshape(total)
    gain_one = params[:, :, :small].reshape(-1).astype(f32)
    gain_two = params[:, :, small : 2 * small].reshape(-1).astype(f32)
    full_ab = params[:, :, 2 * small :].reshape(depth, 2 * HEADS)
    ffn = jnp.concatenate(
        [jnp.where(even, got_one, got_two), jnp.where(even, got_two, got_one), w_down.T], axis=1
    )
    ffn = lax.all_gather(ffn, "seq", axis=0, tiled=True)
    cot_late, _ = lax.optimization_barrier((cot, unit_og))
    cot_all = pair_gather(cot_late, "dp")
    full_gu, full_down_t = ffn[:, : 2 * half], ffn[:, 2 * half :]

    x_f = x_all.astype(f32)
    inv_one = lax.rsqrt(jnp.mean(x_f * x_f, axis=-1, keepdims=True) + EPS)
    normed = (x_f * inv_one * gain_one).astype(bf16)
    columns = jnp.concatenate([unit_qkv, unit_og], axis=1)
    projected = jnp.dot(normed, columns, preferred_element_type=f32)
    channels = 2 * DK + wide
    proj = projected[:, :channels].astype(bf16).astype(f32)
    proj_og = projected[:, channels:]
    pick = (
        jnp.arange(2 * HEADS)[:, None] == jnp.stack([heads.head, heads.head + HEADS])[None]
    ).astype(f32)
    unit_ab = jnp.dot(full_ab.astype(f32), pick).astype(bf16)
    proj_ab = jnp.dot(normed, unit_ab, preferred_element_type=f32)
    ext_ids = jnp.concatenate([jnp.full((CONV - 1,), -1, jnp.int32), seg_ids])
    same = jnp.stack([ext_ids[i : i + total] == seg_ids for i in range(CONV)], axis=1).astype(f32)
    at_head = jnp.arange(HEADS) == heads.head
    own_log = jnp.sum(jnp.where(at_head, a_log, 0.0))
    own_bias = jnp.sum(jnp.where(at_head, dt_bias, 0.0))
    mixed, core_back = jax.vjp(
        lambda *a: unit_core(*a, same, seg_ids),
        proj,
        unit_taps.astype(f32),
        proj_ab,
        own_log,
        own_bias,
    )
    own_gain = lax.dynamic_slice_in_dim(o_gain, heads.part * wide, wide)
    gated_f, gate_back = jax.vjp(
        lambda *a: out_gate(*a, groups), mixed, proj_og, own_gain
    )
    gated = gated_f.astype(bf16)
    gated_rows = exchange(gated.reshape(nseq, length, wide), "seq")
    gated_rows = jnp.swapaxes(gated_rows, 0, 1).reshape(length, nseq * wide)
    quarter = nseq * wide // ndp
    gated_all = []
    for offset in pair_offsets("dp"):
        piece = lax.dynamic_slice_in_dim(
            gated_rows, (lax.axis_index("dp") ^ offset) * quarter, quarter, 1
        )
        gated_all.append(piece if offset == 0 else swap(piece, "dp", offset))
    gated_all = jnp.concatenate(gated_all, axis=0)

    resid = rows.astype(f32) + jnp.dot(gated_rows, full_o, preferred_element_type=f32)
    normed2_f, rms2_back = jax.vjp(rms, resid, gain_two)
    normed2 = pair_gather(normed2_f.astype(bf16), "dp")
    joined = jnp.dot(normed2, full_gu, preferred_element_type=f32)
    act_f, act_back = jax.vjp(swiglu, joined[:, :half], joined[:, half:])
    act = act_f.astype(bf16)
    d_act = jnp.dot(cot_all, full_down_t, preferred_element_type=f32)
    d_gate, d_up = act_back(d_act)
    d_joined = jnp.concatenate([d_gate.astype(bf16), d_up.astype(bf16)], axis=1)
    d_normed2 = pair_scatter(
        jnp.einsum("lf,df->ld", d_joined, full_gu, preferred_element_type=f32), "dp"
    )
    d_resid_n, grad_g2 = rms2_back(d_normed2)
    d_resid = cot.astype(f32) + d_resid_n
    d_resid_b = d_resid.astype(bf16)
    out_part = jnp.einsum("lf,df->ld", act, full_down_t, preferred_element_type=f32)
    out = (resid + pair_scatter(out_part, "dp")).astype(bf16)
    grad_o = jnp.einsum(
        "lv,ld->vd", gated_all, pair_gather(d_resid_b, "dp"), preferred_element_type=f32
    ).reshape(nseq, quarter // nseq, depth)
    pieces = depth // quarter
    grad_o = jnp.concatenate(
        [grad_o[:, :, i * quarter : (i + 1) * quarter] for i in range(pieces)], axis=1
    )
    grad_ffn = jnp.concatenate(
        [
            jnp.einsum("ld,lf->df", normed2, d_joined, preferred_element_type=f32),
            jnp.einsum("ld,lf->df", cot_all, act, preferred_element_type=f32),
            grad_o.reshape(depth, quarter),
        ],
        axis=1,
    ).astype(bf16)
    grad_ffn = lax.psum_scatter(grad_ffn, "seq", scatter_dimension=0, tiled=True)
    grad_down = grad_ffn[:, 2 * half : 3 * half].T.astype(f32)
    grad_o = grad_ffn[:, 3 * half :].astype(f32).reshape(pieces, quarter // nseq, quarter)
    grad_o = jnp.swapaxes(grad_o, 0, 1).reshape(quarter // nseq, depth)
    g_gate, g_up = grad_ffn[:, :half], grad_ffn[:, half : 2 * half]

    d_gated_rows = jnp.einsum("ld,vd->lv", d_resid_b, full_o, preferred_element_type=f32)
    d_gated_rows = jnp.swapaxes(d_gated_rows.astype(bf16).reshape(length, nseq, wide), 0, 1)
    d_gated = exchange(d_gated_rows, "seq").reshape(total, wide).astype(f32)
    d_mixed, d_og, grad_ogain = gate_back(d_gated)
    d_proj, d_taps, d_ab, d_log, d_bias = core_back(d_mixed)
    d_columns = jnp.concatenate([d_proj.astype(bf16), d_og.astype(bf16)], axis=1)
    d_ab_b = d_ab.astype(bf16)
    d_normed_part = jnp.einsum(
        "lc,dc->ld", d_columns, columns, preferred_element_type=f32
    ) + jnp.einsum("lc,dc->ld", d_ab_b, unit_ab, preferred_element_type=f32)
    grad_g1 = jnp.sum(d_normed_part * (x_f * inv_one), axis=0)
    grad_columns = jnp.einsum(
        "ld,lc->dc", normed, d_columns, preferred_element_type=f32
    ).astype(bf16)
    grad_ab = jnp.einsum("ld,lc->dc", normed, d_ab_b, preferred_element_type=f32)
    grad_ab = jnp.dot(grad_ab, pick.T, precision=HIGH)
    owned = jnp.concatenate(
        [
            grad_g1.reshape(ndp, nseq, small),
            grad_g2.reshape(ndp, nseq, small),
            grad_ab.reshape(ndp, nseq, small * 2 * HEADS),
        ],
        axis=2,
    )
    owned = jnp.swapaxes(relative(owned, "dp"), 0, 1)
    owned = relative(owned, "seq")
    shared = jnp.concatenate(
        [
            jnp.where(at_head, d_log, 0.0),
            jnp.where(at_head, d_bias, 0.0),
            lax.dynamic_update_slice_in_dim(
                jnp.zeros((DV,), f32), grad_ogain, heads.part * wide, 0
            ),
        ]
    )
    count = shared.shape[0]

    def shared_job():
        mine, everyones = owned, shared
        for axis in ("seq", "dp"):
            for bit in pair_bits(axis):
                half = mine.shape[0] // 2
                sent = jnp.concatenate([mine[half:].reshape(-1), everyones])
                (got,) = yield (swap(sent, axis, bit),)
                mine = mine[:half] + got[:-count].reshape(mine[:half].shape)
                everyones = everyones + got[-count:]
            mine = mine[0]
        return jnp.concatenate([mine, everyones])

    def ffn_back_job():
        for _ in range(3):
            yield ()
        one, two = jnp.where(even, g_gate, g_up), jnp.where(even, g_up, g_gate)
        return (
            yield (
                lax.ppermute(one, "dp", heads.back(round_one)),
                lax.ppermute(two, "dp", heads.back(round_two)),
            )
        )

    d_normed, (grad_qkv, grad_conv, grad_og), owned, (back_one, back_two) = together(
        ring_scatter_job(d_normed_part.reshape(nseq, length, depth), "seq"),
        heads.give(grad_columns[:, :channels], d_taps, grad_columns[:, channels:]),
        shared_job(),
        ffn_back_job(),
    )
    grad_gu = jnp.where(
        low_half,
        jnp.concatenate([back_one, back_two], axis=1),
        jnp.concatenate([back_two, back_one], axis=1),
    ).astype(f32)
    _, rms1_back = jax.vjp(lambda r: rms(r, gain_one), rows.astype(f32))
    (d_rows_n,) = rms1_back(d_normed)
    d_rows = (d_resid + d_rows_n).astype(bf16)
    return (
        out[None],
        d_rows[None],
        owned[:small],
        grad_qkv,
        owned[2 * small : -count].reshape(small, 2 * HEADS),
        grad_og,
        grad_conv,
        owned[-count:][:HEADS],
        owned[-count:][HEADS : 2 * HEADS],
        owned[-count:][2 * HEADS :],
        grad_o,
        owned[small : 2 * small],
        grad_gu,
        grad_down,
    )


def solution(mesh):
    return jax.shard_map(
        local,
        mesh=mesh,
        in_specs=(
            P("dp", "seq", None),
            P("dp", "seq"),
            P(("dp", "seq")),
            P(None, ("dp", "seq")),
            P(("dp", "seq"), None),
            P(None, ("dp", "seq")),
            P(None, ("dp", "seq")),
            P(),
            P(),
            P(),
            P(("dp", "seq"), None),
            P(("dp", "seq")),
            P("seq", "dp"),
            P("dp", "seq"),
            P("dp", "seq", None),
        ),
        out_specs=(
            P("dp", "seq", None),
            P("dp", "seq", None),
            P(("dp", "seq")),
            P(None, ("dp", "seq")),
            P(("dp", "seq"), None),
            P(None, ("dp", "seq")),
            P(None, ("dp", "seq")),
            P(),
            P(),
            P(),
            P(("dp", "seq"), None),
            P(("dp", "seq")),
            P("seq", "dp"),
            P("dp", "seq"),
        ),
        check_vma=False,
    )
```

```python
import functools

import jax
import jax.numpy as jnp
from jax import lax
from jax.experimental import pallas as pl
from jax.experimental.pallas import tpu as pltpu
from jax.sharding import PartitionSpec as P

HEADS = 8
DK = 128
DV = 256
CONV = 4
BLOCK = 64
EDGE = 16
EPS = 1e-06
BOTH = ("dp", "seq")


f32 = jnp.float32
bf16 = jnp.bfloat16
HIGH = lax.Precision.HIGHEST


def rms(values, gain):
    return values * lax.rsqrt(jnp.mean(values * values, axis=-1, keepdims=True) + EPS) * gain


def swiglu(gate, up):
    return jax.nn.silu(gate) * up


def convolve(extended, weights, same):
    length = same.shape[0]
    total = jnp.zeros((length, extended.shape[1]), f32)
    for i in range(CONV):
        total = total + weights[i] * extended[i : i + length] * same[:, i : i + 1]
    return jax.nn.silu(total)


def exchange(blocks, axis):
    return lax.all_to_all(blocks, axis, 0, 0)


def spread(value, axis):
    count = lax.axis_size(axis)
    return exchange(jnp.broadcast_to(value[None], (count,) + value.shape), axis)


def swap(value, axis, bit):
    count = lax.axis_size(axis)
    return lax.ppermute(value, axis, [(i, i ^ bit) for i in range(count)])


def pair_bits(axis):
    count = lax.axis_size(axis)
    bits, bit = [], 1
    while bit < count:
        bits.append(bit)
        bit *= 2
    return bits


def pair_gather(rows, axis):
    for bit in reversed(pair_bits(axis)):
        rows = jnp.concatenate([rows, swap(rows, axis, bit)], axis=0)
    return rows


def pair_scatter(rows, axis, kind=bf16):
    for bit in pair_bits(axis):
        half = rows.shape[0] // 2
        rows = rows[:half].astype(f32) + swap(rows[half:].astype(kind), axis, bit).astype(f32)
    return rows


def pair_offsets(axis):
    offsets = [0]
    for bit in reversed(pair_bits(axis)):
        offsets = offsets + [offset ^ bit for offset in offsets]
    return offsets


def lookup(table, index):
    return sum(entry * (index == i).astype(jnp.int32) for i, entry in enumerate(table))


def ring_order(count):
    return list(range(0, count, 2)) + list(range(count - 1, 0, -2))


def ring_pairs(count, turn):
    order = ring_order(count)
    return [(order[r], order[(r + turn) % count]) for r in range(count)]


def ring_place(axis):
    count = lax.axis_size(axis)
    order = ring_order(count)
    place = [order.index(i) for i in range(count)]
    at = lookup(place, lax.axis_index(axis))
    return lambda ahead: lookup(order, (at + ahead + count) % count)


def together(*jobs):
    results = [None] * len(jobs)
    waiting = {}
    for i, job in enumerate(jobs):
        try:
            waiting[i] = next(job)
        except StopIteration as stop:
            results[i] = stop.value
    while waiting:
        waiting = lax.optimization_barrier(waiting)
        later = {}
        for i, received in waiting.items():
            try:
                later[i] = jobs[i].send(received)
            except StopIteration as stop:
                results[i] = stop.value
        waiting = later
    return results


def pair_gather_job(rows, axis):
    for bit in reversed(pair_bits(axis)):
        (other,) = yield (swap(rows, axis, bit),)
        rows = jnp.concatenate([rows, other], axis=0)
    return rows


def pair_scatter_job(rows, axis):
    for bit in pair_bits(axis):
        half = rows.shape[0] // 2
        (other,) = yield (swap(rows[half:].astype(bf16), axis, bit),)
        rows = rows[:half].astype(f32) + other.astype(f32)
    return rows


def ring_gather_job(block, axis, rows):
    count = lax.axis_size(axis)
    source = ring_place(axis)
    whole = jnp.zeros((count * rows, block.shape[1]), block.dtype)
    tails = jnp.zeros((count, 1, block.shape[1]), block.dtype)

    def put(whole, tails, got, ahead):
        at = source(ahead)
        return (
            lax.dynamic_update_slice_in_dim(whole, got[:rows], at * rows, 0),
            jnp.where(jnp.arange(count)[:, None, None] == at, got[rows : rows + 1][None], tails),
        )

    whole, tails = put(whole, tails, block, 0)
    one = two = block
    for k in range(1, count // 2 + 1):
        both = k < count - count // 2
        one = lax.ppermute(one, axis, ring_pairs(count, 1))
        if both:
            two = lax.ppermute(two, axis, ring_pairs(count, -1))
            one, two = yield (one, two)
            whole, tails = put(whole, tails, two, k)
        else:
            (one,) = yield (one,)
        whole, tails = put(whole, tails, one, -k)
    return whole, tails[:, 0]


def relative(values, axis):
    count = lax.axis_size(axis)
    wanted = jnp.asarray(pair_offsets(axis), jnp.int32) ^ lax.axis_index(axis)
    pick = wanted[:, None] == jnp.arange(count)[None]
    pick = pick.reshape(pick.shape + (1,) * (values.ndim - 1))
    return jnp.sum(jnp.where(pick, values[None], jnp.zeros((), values.dtype)), axis=1)


def absolute(values, axis):
    count = lax.axis_size(axis)
    wanted = jnp.asarray(pair_offsets(axis), jnp.int32) ^ lax.axis_index(axis)
    pick = jnp.arange(count)[:, None] == wanted[None]
    pick = pick.reshape(pick.shape + (1,) * (values.ndim - 1))
    return jnp.sum(jnp.where(pick, values[None], jnp.zeros((), values.dtype)), axis=1)


def ring_scatter_job(parts, axis):
    count = lax.axis_size(axis)
    source = ring_place(axis)
    part = lambda ahead: lax.dynamic_index_in_dim(parts, source(ahead), 0, keepdims=False)
    far = count // 2
    near = count - 1 - far
    one, two = part(far).astype(bf16), part(-near).astype(bf16)
    for k in range(far):
        one = lax.ppermute(one, axis, ring_pairs(count, 1))
        if k < near:
            two = lax.ppermute(two, axis, ring_pairs(count, -1))
        one, two = yield (one, two)
        if k < far - 1:
            one = (one.astype(f32) + part(far - k - 1)).astype(bf16)
        if k < near - 1:
            two = (two.astype(f32) + part(-(near - k - 1))).astype(bf16)
    return part(0) + one.astype(f32) + two.astype(f32)


def split_dot(a, b):
    a_hi, b_hi = a.astype(bf16), b.astype(bf16)
    a_lo = (a - a_hi.astype(f32)).astype(bf16)
    b_lo = (b - b_hi.astype(f32)).astype(bf16)
    dot = functools.partial(jnp.dot, preferred_element_type=f32)
    return dot(a_hi, b_hi) + (dot(a_hi, b_lo) + dot(a_lo, b_hi))


def chain_forward(m_ref, b_ref, s_ref):
    blocks, _, width = b_ref.shape

    def step(c, state):
        s_ref[c] = state
        return split_dot(m_ref[c], state) + b_ref[c]

    lax.fori_loop(0, blocks, step, jnp.zeros((DK, width), f32))


def chain_backward(mt_ref, d_ref, g_ref):
    blocks, _, width = d_ref.shape

    def step(i, grad):
        c = blocks - 1 - i
        g_ref[c] = grad
        return split_dot(mt_ref[c], grad) + d_ref[c]

    lax.fori_loop(0, blocks, step, jnp.zeros((DK, width), f32))


def run_chain(kernel, maps, terms):
    width = terms.shape[2]
    terms = jnp.pad(terms, ((0, 0), (0, 0), (0, -width % 128)))
    return pl.pallas_call(
        kernel,
        out_shape=jax.ShapeDtypeStruct(terms.shape, f32),
        in_specs=[pl.BlockSpec(memory_space=pltpu.VMEM)] * 2,
        out_specs=pl.BlockSpec(memory_space=pltpu.VMEM),
    )(maps, terms)[:, :, :width]


@jax.custom_vjp
def chain(maps, terms):
    return run_chain(chain_forward, maps, terms)


def chain_fwd(maps, terms):
    states = run_chain(chain_forward, maps, terms)
    return states, (maps, states)


def chain_bwd(saved, d_states):
    maps, states = saved
    grads = run_chain(chain_backward, jnp.swapaxes(maps, 1, 2), d_states)
    return jnp.einsum("ndv,nev->nde", grads, states, preferred_element_type=f32, precision=HIGH), grads


chain.defvjp(chain_fwd, chain_bwd)


def bdot(a, b, precision=HIGH):
    return jnp.einsum("nij,njk->nik", a, b, precision=precision, preferred_element_type=f32)


def inverse_of(strict_lower):
    size = strict_lower.shape[-1]
    rows_i = lax.broadcasted_iota(jnp.int32, (size, size), 0)
    cols_j = lax.broadcasted_iota(jnp.int32, (size, size), 1)
    inverse = jnp.broadcast_to(jnp.eye(size, dtype=f32), strict_lower.shape)
    width = 1
    while width < size:
        inside = (rows_i // (2 * width) == cols_j // (2 * width)) & (
            rows_i // width != cols_j // width
        )
        part = jnp.where(inside, strict_lower, 0.0)
        if width == 1:
            inverse = inverse - part
        else:
            inverse = inverse - bdot(bdot(inverse, part, HIGH), inverse, HIGH)
        width *= 2
    return inverse


@jax.custom_vjp
def unit_inverse(strict_lower):
    return inverse_of(strict_lower)


def unit_inverse_fwd(strict_lower):
    inverse = inverse_of(strict_lower)
    return inverse, inverse


def unit_inverse_bwd(inverse, d_inverse):
    flipped = jnp.swapaxes(inverse, 1, 2)
    return (-bdot(bdot(flipped, d_inverse, HIGH), flipped, HIGH),)


unit_inverse.defvjp(unit_inverse_fwd, unit_inverse_bwd)


def head_rule(queries, keys, values, betas, decays, seg_ids):
    length = queries.shape[0]
    size = min(BLOCK, length)
    blocks = length // size
    q = queries.reshape(blocks, size, DK)
    k = keys.reshape(blocks, size, DK)
    v = values.reshape(blocks, size, -1)
    beta = betas.reshape(blocks, size)
    seg = seg_ids.reshape(blocks, size)
    prev = jnp.concatenate([jnp.full((1,), -1, seg.dtype), seg[:-1, -1]])
    rows_i = lax.broadcasted_iota(jnp.int32, (size, size), 0)
    cols_j = lax.broadcasted_iota(jnp.int32, (size, size), 1)
    upto = (rows_i <= cols_j).astype(f32)
    gamma = jnp.dot(decays.reshape(blocks, size), upto, precision=HIGH)
    same = seg[:, :, None] == seg[:, None, :]
    incl = jnp.logical_and(same, (cols_j <= rows_i)[None])
    strict = jnp.logical_and(same, (cols_j < rows_i)[None]).astype(f32)
    diff = gamma[:, :, None] - gamma[:, None, :]
    lower = jnp.where(incl, jnp.exp(jnp.where(incl, diff, 0.0)), 0.0)
    carry_in = (seg == prev[:, None]).astype(f32)
    scaled = jnp.exp(gamma) * carry_in
    key_dots = jnp.einsum("nid,njd->nij", k, k, precision=HIGH)
    inverse = unit_inverse(beta[:, :, None] * lower * strict * key_dots)
    sides = jnp.concatenate([beta[:, :, None] * v, (beta * scaled)[:, :, None] * k], axis=2)
    fresh = bdot(inverse, sides, HIGH)
    new_v, new_k = fresh[:, :, : v.shape[2]], fresh[:, :, v.shape[2] :]
    scores = jnp.einsum("nid,njd->nij", q, k, precision=HIGH) * lower
    q_tilde = q * scaled[:, :, None] - bdot(scores, new_k)
    o_new = bdot(scores, new_v)
    tail = jnp.exp(gamma[:, -1:] - gamma) * (seg == seg[:, -1:]).astype(f32)
    key_tail = k * tail[:, :, None]
    keep = (jnp.exp(gamma[:, -1]) * carry_in[:, -1])[:, None, None]
    m_map = keep * jnp.eye(DK, dtype=f32)[None] - jnp.einsum("njd,nje->nde", key_tail, new_k, precision=HIGH)
    b_map = jnp.einsum("njd,njv->ndv", key_tail, new_v, precision=HIGH)
    states = chain(m_map, b_map)
    return (o_new + bdot(q_tilde, states)).reshape(length, -1)


def unit_core(proj, taps, proj_ab, a_log, dt_bias, same, seg_ids):
    extended = jnp.concatenate([jnp.zeros((CONV - 1, proj.shape[1]), f32), proj], axis=0)
    conv_out = convolve(extended, taps, same)
    queries = conv_out[:, :DK]
    keys = conv_out[:, DK : 2 * DK]
    values = conv_out[:, 2 * DK :]
    queries = (
        queries * lax.rsqrt(jnp.sum(queries * queries, axis=-1, keepdims=True) + EPS) * DK ** (-0.5)
    )
    keys = keys * lax.rsqrt(jnp.sum(keys * keys, axis=-1, keepdims=True) + EPS)
    betas = jax.nn.sigmoid(proj_ab[:, 0])
    decays = -jnp.exp(a_log) * jax.nn.softplus(proj_ab[:, 1] + dt_bias)
    return head_rule(queries, keys, values, betas, decays, seg_ids)


def out_gate(mixed, proj_og, gain, groups):
    squares = jnp.sum(mixed * mixed, axis=-1, keepdims=True)
    if groups is not None:
        squares = lax.psum(squares, "seq", axis_index_groups=groups)
    return mixed * lax.rsqrt(squares / DV + EPS) * gain * jax.nn.silu(proj_og)


class Heads:
    def __init__(self, w_qkv, w_og):
        self.ndp = lax.axis_size("dp")
        self.nseq = lax.axis_size("seq")
        self.split = self.nseq // HEADS
        self.wide = DV // self.split
        unit = lax.axis_index("seq")
        self.head = unit // self.split
        self.part = unit % self.split
        self.cq = w_qkv.shape[1]
        self.co = w_og.shape[1]
        self.direct = (
            self.split == 1
            and DK % self.cq == 0
            and (2 * DK + DV) == self.ndp * self.cq
            and DV == self.ndp * self.co
            and 2 * self.co == self.cq
        )
        if self.direct:
            per = DK // self.cq
            self.to_qkv, self.to_og = [], []
            for j in range(self.ndp * self.nseq):
                kind, head, place = 0, j // per, j % per
                if head >= HEADS:
                    kind, head = 1, head - HEADS
                if head >= HEADS:
                    own = j - 2 * HEADS * per
                    kind, head, place = 2, own // (DV // self.cq), own % (DV // self.cq)
                slot = kind * per + place
                self.to_qkv.append((j, slot * self.nseq + head))
                self.to_og.append((j, (j % self.ndp) * self.nseq + j // self.ndp))

    def back(self, pairs):
        return [(b, a) for a, b in pairs]

    def starts(self):
        base = 2 * HEADS * DK
        return (
            (self.head * DK, DK),
            ((HEADS + self.head) * DK, DK),
            (base + self.head * DV + self.part * self.wide, self.wide),
        )

    def fetch(self, w_qkv, conv_w, w_og):
        if not self.direct:
            full = lax.all_gather(w_qkv, BOTH, axis=1, tiled=True)
            taps = lax.all_gather(conv_w, BOTH, axis=1, tiled=True)
            gates = lax.all_gather(w_og, BOTH, axis=1, tiled=True)
            take = lambda a: jnp.concatenate(
                [lax.dynamic_slice_in_dim(a, s, n, 1) for s, n in self.starts()], axis=1
            )
            og = lax.dynamic_slice_in_dim(
                gates, self.head * DV + self.part * self.wide, self.wide, 1
            )
            return take(full), take(taps), og
        depth = w_qkv.shape[0]
        half = depth // 2
        padded = jnp.pad(conv_w, ((0, EDGE - CONV), (0, 0)))
        one = lax.ppermute(jnp.concatenate([w_qkv, padded], axis=0), BOTH, self.to_qkv)
        two = lax.ppermute(
            jnp.concatenate([w_og[:half], w_og[half:]], axis=1), BOTH, self.to_og
        )
        one, two = yield (one, two)
        mine = jnp.concatenate([one, two], axis=0)
        offsets = pair_offsets("dp")
        relative = yield from pair_gather_job(mine, "dp")
        relative = relative.reshape((self.ndp,) + mine.shape)
        places = [offsets.index(i) for i in range(self.ndp)]
        here = lax.axis_index("dp")
        all_slots = jnp.stack(
            [
                lax.dynamic_index_in_dim(relative, lookup(places, here ^ s), 0, keepdims=False)
                for s in range(self.ndp)
            ]
        )
        qkv = jnp.concatenate([all_slots[s, :depth] for s in range(self.ndp)], axis=1)
        taps = jnp.concatenate(
            [all_slots[s, depth : depth + CONV] for s in range(self.ndp)], axis=1
        )
        low = all_slots[:, depth + EDGE :]
        og = jnp.concatenate(
            [
                jnp.concatenate([low[s, :, : self.co], low[s, :, self.co :]], axis=0)
                for s in range(self.ndp)
            ],
            axis=1,
        )
        return qkv, taps, og

    def give(self, d_qkv, d_taps, d_og):
        depth = d_qkv.shape[0]
        half = depth // 2
        if not self.direct:
            outs = []
            for grad, total in ((d_qkv, 2 * HEADS * DK + HEADS * DV), (d_taps, None)):
                total = 2 * HEADS * DK + HEADS * DV
                full = jnp.zeros((grad.shape[0], total), f32)
                at = 0
                for start, n in self.starts():
                    full = lax.dynamic_update_slice_in_dim(
                        full, grad[:, at : at + n].astype(f32), start, 1
                    )
                    at += n
                outs.append(
                    lax.psum_scatter(full.astype(bf16), BOTH, scatter_dimension=1, tiled=True)
                )
            full = lax.dynamic_update_slice_in_dim(
                jnp.zeros((depth, HEADS * DV), f32),
                d_og.astype(f32),
                self.head * DV + self.part * self.wide,
                1,
            )
            og = lax.psum_scatter(full.astype(bf16), BOTH, scatter_dimension=1, tiled=True)
            return outs[0].astype(f32), outs[1].astype(f32), og.astype(f32)
        cq, co = self.cq, self.co
        taps = jnp.pad(d_taps.astype(bf16), ((0, EDGE - CONV), (0, 0)))
        blocks = jnp.stack(
            [
                jnp.concatenate(
                    [
                        d_qkv[:, s * cq : (s + 1) * cq],
                        taps[:, s * cq : (s + 1) * cq],
                        jnp.concatenate(
                            [
                                d_og[:half, s * co : (s + 1) * co],
                                d_og[half:, s * co : (s + 1) * co],
                            ],
                            axis=1,
                        ),
                    ],
                    axis=0,
                )
                for s in range(self.ndp)
            ]
        )
        here = lax.axis_index("dp")
        blocks = jnp.concatenate(
            [
                lax.dynamic_index_in_dim(blocks, here ^ offset, 0, keepdims=False)
                for offset in pair_offsets("dp")
            ],
            axis=0,
        )
        yield ()
        summed = (yield from pair_scatter_job(blocks, "dp")).astype(bf16)
        one = lax.ppermute(summed[: depth + EDGE], BOTH, self.back(self.to_qkv))
        two = lax.ppermute(summed[depth + EDGE :], BOTH, self.back(self.to_og))
        one, two = yield (one, two)
        one, two = one.astype(f32), two.astype(f32)
        return (
            one[:depth],
            one[depth : depth + CONV],
            jnp.concatenate([two[:, :co], two[:, co:]], axis=0),
        )


def halves_rounds(count):
    first, second = [], []
    for p in range(count):
        low = p < count // 2
        base = 2 * (p if low else p - count // 2)
        first.append((p, base if low else base + 1))
        second.append((p, base + 1 if low else base))
    return first, second


def local(
    block_input,
    segment_ids,
    norm_gain,
    w_qkv,
    w_ab,
    w_og,
    conv_w,
    a_log,
    dt_bias,
    o_gain,
    w_o,
    mlp_gain,
    w_gu,
    w_down,
    cotangent,
):
    heads = Heads(w_qkv, w_og)
    ndp, nseq, split, wide = heads.ndp, heads.nseq, heads.split, heads.wide
    rows = block_input[0]
    cot = cotangent[0]
    length, depth = rows.shape
    total = length * nseq
    small = norm_gain.shape[0]
    groups = None
    if split > 1:
        groups = [[h * split + i for i in range(split)] for h in range(HEADS)]

    full_o = lax.all_gather(w_o, BOTH, axis=0, tiled=True)
    half = w_gu.shape[1] // 2
    round_one, round_two = halves_rounds(ndp)
    low_half = lax.axis_index("dp") < ndp // 2
    even = lax.axis_index("dp") % 2 == 0

    def input_job():
        extra = jnp.concatenate(
            [norm_gain, mlp_gain, w_ab.reshape(-1), segment_ids[0].astype(bf16)]
        )
        used = extra.shape[0]
        extra = jnp.pad(extra, (0, EDGE * depth - used)).reshape(EDGE, depth)
        whole, tails = yield from ring_gather_job(
            jnp.concatenate([rows, extra], axis=0), "seq", length
        )
        params = yield from pair_gather_job(tails[None, :, : used - length], "dp")
        return whole, tails[:, used - length : used], absolute(params, "dp")

    def ffn_job():
        yield ()
        one = lax.ppermute(jnp.where(low_half, w_gu[:, :half], w_gu[:, half:]), "dp", round_one)
        two = lax.ppermute(jnp.where(low_half, w_gu[:, half:], w_gu[:, :half]), "dp", round_two)
        return (yield (one, two))

    (x_all, seg_ids, params), (unit_qkv, unit_taps, unit_og), (got_one, got_two) = together(
        input_job(), heads.fetch(w_qkv, conv_w, w_og), ffn_job()
    )
    seg_ids = seg_ids.astype(jnp.int32).reshape(total)
    gain_one = params[:, :, :small].reshape(-1).astype(f32)
    gain_two = params[:, :, small : 2 * small].reshape(-1).astype(f32)
    full_ab = params[:, :, 2 * small :].reshape(depth, 2 * HEADS)
    ffn = jnp.concatenate(
        [jnp.where(even, got_one, got_two), jnp.where(even, got_two, got_one), w_down.T], axis=1
    )
    ffn = lax.all_gather(ffn, "seq", axis=0, tiled=True)
    cot_late, _ = lax.optimization_barrier((cot, unit_og))
    cot_all = pair_gather(cot_late, "dp")
    full_gu, full_down_t = ffn[:, : 2 * half], ffn[:, 2 * half :]

    x_f = x_all.astype(f32)
    inv_one = lax.rsqrt(jnp.mean(x_f * x_f, axis=-1, keepdims=True) + EPS)
    normed = (x_f * inv_one * gain_one).astype(bf16)
    columns = jnp.concatenate([unit_qkv, unit_og], axis=1)
    projected = jnp.dot(normed, columns, preferred_element_type=f32)
    channels = 2 * DK + wide
    proj = projected[:, :channels].astype(bf16).astype(f32)
    proj_og = projected[:, channels:]
    pick = (
        jnp.arange(2 * HEADS)[:, None] == jnp.stack([heads.head, heads.head + HEADS])[None]
    ).astype(f32)
    unit_ab = jnp.dot(full_ab.astype(f32), pick).astype(bf16)
    proj_ab = jnp.dot(normed, unit_ab, preferred_element_type=f32)
    ext_ids = jnp.concatenate([jnp.full((CONV - 1,), -1, jnp.int32), seg_ids])
    same = jnp.stack([ext_ids[i : i + total] == seg_ids for i in range(CONV)], axis=1).astype(f32)
    at_head = jnp.arange(HEADS) == heads.head
    own_log = jnp.sum(jnp.where(at_head, a_log, 0.0))
    own_bias = jnp.sum(jnp.where(at_head, dt_bias, 0.0))
    mixed, core_back = jax.vjp(
        lambda *a: unit_core(*a, same, seg_ids),
        proj,
        unit_taps.astype(f32),
        proj_ab,
        own_log,
        own_bias,
    )
    own_gain = lax.dynamic_slice_in_dim(o_gain, heads.part * wide, wide)
    gated_f, gate_back = jax.vjp(
        lambda *a: out_gate(*a, groups), mixed, proj_og, own_gain
    )
    gated = gated_f.astype(bf16)
    gated_rows = exchange(gated.reshape(nseq, length, wide), "seq")
    gated_rows = jnp.swapaxes(gated_rows, 0, 1).reshape(length, nseq * wide)
    quarter = nseq * wide // ndp
    gated_all = []
    for offset in pair_offsets("dp"):
        piece = lax.dynamic_slice_in_dim(
            gated_rows, (lax.axis_index("dp") ^ offset) * quarter, quarter, 1
        )
        gated_all.append(piece if offset == 0 else swap(piece, "dp", offset))
    gated_all = jnp.concatenate(gated_all, axis=0)

    resid = rows.astype(f32) + jnp.dot(gated_rows, full_o, preferred_element_type=f32)
    normed2_f, rms2_back = jax.vjp(rms, resid, gain_two)
    normed2 = pair_gather(normed2_f.astype(bf16), "dp")
    joined = jnp.dot(normed2, full_gu, preferred_element_type=f32)
    act_f, act_back = jax.vjp(swiglu, joined[:, :half], joined[:, half:])
    act = act_f.astype(bf16)
    d_act = jnp.dot(cot_all, full_down_t, preferred_element_type=f32)
    d_gate, d_up = act_back(d_act)
    d_joined = jnp.concatenate([d_gate.astype(bf16), d_up.astype(bf16)], axis=1)
    d_normed2 = pair_scatter(
        jnp.einsum("lf,df->ld", d_joined, full_gu, preferred_element_type=f32), "dp", f32
    )
    d_resid_n, grad_g2 = rms2_back(d_normed2)
    d_resid = cot.astype(f32) + d_resid_n
    d_resid_b = d_resid.astype(bf16)
    out_part = jnp.einsum("lf,df->ld", act, full_down_t, preferred_element_type=f32)
    out = (resid + pair_scatter(out_part, "dp")).astype(bf16)
    grad_o = jnp.einsum(
        "lv,ld->vd", gated_all, pair_gather(d_resid_b, "dp"), preferred_element_type=f32
    ).reshape(nseq, quarter // nseq, depth)
    pieces = depth // quarter
    grad_o = jnp.concatenate(
        [grad_o[:, :, i * quarter : (i + 1) * quarter] for i in range(pieces)], axis=1
    )
    grad_ffn = jnp.concatenate(
        [
            jnp.einsum("ld,lf->df", normed2, d_joined, preferred_element_type=f32),
            jnp.einsum("ld,lf->df", cot_all, act, preferred_element_type=f32),
            grad_o.reshape(depth, quarter),
        ],
        axis=1,
    ).astype(bf16)
    grad_ffn = lax.psum_scatter(grad_ffn, "seq", scatter_dimension=0, tiled=True)
    grad_down = grad_ffn[:, 2 * half : 3 * half].T.astype(f32)
    grad_o = grad_ffn[:, 3 * half :].astype(f32).reshape(pieces, quarter // nseq, quarter)
    grad_o = jnp.swapaxes(grad_o, 0, 1).reshape(quarter // nseq, depth)
    g_gate, g_up = grad_ffn[:, :half], grad_ffn[:, half : 2 * half]

    d_gated_rows = jnp.einsum("ld,vd->lv", d_resid_b, full_o, preferred_element_type=f32)
    d_gated_rows = jnp.swapaxes(d_gated_rows.reshape(length, nseq, wide), 0, 1)
    d_gated = exchange(d_gated_rows, "seq").reshape(total, wide)
    d_mixed, d_og, grad_ogain = gate_back(d_gated)
    d_proj, d_taps, d_ab, d_log, d_bias = core_back(d_mixed)
    d_columns = jnp.concatenate([d_proj.astype(bf16), d_og.astype(bf16)], axis=1)
    d_ab_b = d_ab.astype(bf16)
    d_normed_part = jnp.einsum(
        "lc,dc->ld", d_columns, columns, preferred_element_type=f32
    ) + jnp.einsum("lc,dc->ld", d_ab_b, unit_ab, preferred_element_type=f32)
    grad_g1 = jnp.sum(d_normed_part * (x_f * inv_one), axis=0)
    grad_columns = jnp.einsum(
        "ld,lc->dc", normed, d_columns, preferred_element_type=f32
    ).astype(bf16)
    grad_ab = jnp.einsum("ld,lc->dc", normed, d_ab_b, preferred_element_type=f32)
    grad_ab = jnp.dot(grad_ab, pick.T, precision=HIGH)
    owned = jnp.concatenate(
        [
            grad_g1.reshape(ndp, nseq, small),
            grad_g2.reshape(ndp, nseq, small),
            grad_ab.reshape(ndp, nseq, small * 2 * HEADS),
        ],
        axis=2,
    )
    owned = jnp.swapaxes(relative(owned, "dp"), 0, 1)
    owned = relative(owned, "seq")
    shared = jnp.concatenate(
        [
            jnp.where(at_head, d_log, 0.0),
            jnp.where(at_head, d_bias, 0.0),
            lax.dynamic_update_slice_in_dim(
                jnp.zeros((DV,), f32), grad_ogain, heads.part * wide, 0
            ),
        ]
    )
    count = shared.shape[0]

    def shared_job():
        mine, everyones = owned, shared
        for axis in ("seq", "dp"):
            for bit in pair_bits(axis):
                half = mine.shape[0] // 2
                sent = jnp.concatenate([mine[half:].reshape(-1), everyones])
                (got,) = yield (swap(sent, axis, bit),)
                mine = mine[:half] + got[:-count].reshape(mine[:half].shape)
                everyones = everyones + got[-count:]
            mine = mine[0]
        return jnp.concatenate([mine, everyones])

    def ffn_back_job():
        for _ in range(3):
            yield ()
        one, two = jnp.where(even, g_gate, g_up), jnp.where(even, g_up, g_gate)
        return (
            yield (
                lax.ppermute(one, "dp", heads.back(round_one)),
                lax.ppermute(two, "dp", heads.back(round_two)),
            )
        )

    d_normed, (grad_qkv, grad_conv, grad_og), owned, (back_one, back_two) = together(
        ring_scatter_job(d_normed_part.reshape(nseq, length, depth), "seq"),
        heads.give(grad_columns[:, :channels], d_taps, grad_columns[:, channels:]),
        shared_job(),
        ffn_back_job(),
    )
    grad_gu = jnp.where(
        low_half,
        jnp.concatenate([back_one, back_two], axis=1),
        jnp.concatenate([back_two, back_one], axis=1),
    ).astype(f32)
    _, rms1_back = jax.vjp(lambda r: rms(r, gain_one), rows.astype(f32))
    (d_rows_n,) = rms1_back(d_normed)
    d_rows = (d_resid + d_rows_n).astype(bf16)
    return (
        out[None],
        d_rows[None],
        owned[:small],
        grad_qkv,
        owned[2 * small : -count].reshape(small, 2 * HEADS),
        grad_og,
        grad_conv,
        owned[-count:][:HEADS],
        owned[-count:][HEADS : 2 * HEADS],
        owned[-count:][2 * HEADS :],
        grad_o,
        owned[small : 2 * small],
        grad_gu,
        grad_down,
    )


def solution(mesh):
    return jax.shard_map(
        local,
        mesh=mesh,
        in_specs=(
            P("dp", "seq", None),
            P("dp", "seq"),
            P(("dp", "seq")),
            P(None, ("dp", "seq")),
            P(("dp", "seq"), None),
            P(None, ("dp", "seq")),
            P(None, ("dp", "seq")),
            P(),
            P(),
            P(),
            P(("dp", "seq"), None),
            P(("dp", "seq")),
            P("seq", "dp"),
            P("dp", "seq"),
            P("dp", "seq", None),
        ),
        out_specs=(
            P("dp", "seq", None),
            P("dp", "seq", None),
            P(("dp", "seq")),
            P(None, ("dp", "seq")),
            P(("dp", "seq"), None),
            P(None, ("dp", "seq")),
            P(None, ("dp", "seq")),
            P(),
            P(),
            P(),
            P(("dp", "seq"), None),
            P(("dp", "seq")),
            P("seq", "dp"),
            P("dp", "seq"),
        ),
        check_vma=False,
    )
```

```python
import functools

import jax
import jax.numpy as jnp
from jax import lax
from jax.experimental import pallas as pl
from jax.experimental.pallas import tpu as pltpu
from jax.sharding import PartitionSpec as P

HEADS = 8
DK = 128
DV = 256
CONV = 4
BLOCK = 128
EDGE = 16
EPS = 1e-06
BOTH = ("dp", "seq")


f32 = jnp.float32
bf16 = jnp.bfloat16
HIGH = lax.Precision.HIGH


def rms(values, gain):
    return values * lax.rsqrt(jnp.mean(values * values, axis=-1, keepdims=True) + EPS) * gain


def swiglu(gate, up):
    return jax.nn.silu(gate) * up


def convolve(extended, weights, same):
    length = same.shape[0]
    total = jnp.zeros((length, extended.shape[1]), f32)
    for i in range(CONV):
        total = total + weights[i] * extended[i : i + length] * same[:, i : i + 1]
    return jax.nn.silu(total)


def exchange(blocks, axis):
    return lax.all_to_all(blocks, axis, 0, 0)


def spread(value, axis):
    count = lax.axis_size(axis)
    return exchange(jnp.broadcast_to(value[None], (count,) + value.shape), axis)


def swap(value, axis, bit):
    count = lax.axis_size(axis)
    return lax.ppermute(value, axis, [(i, i ^ bit) for i in range(count)])


def pair_bits(axis):
    count = lax.axis_size(axis)
    bits, bit = [], 1
    while bit < count:
        bits.append(bit)
        bit *= 2
    return bits


def pair_gather(rows, axis):
    for bit in reversed(pair_bits(axis)):
        rows = jnp.concatenate([rows, swap(rows, axis, bit)], axis=0)
    return rows


def pair_scatter(rows, axis, kind=bf16):
    for bit in pair_bits(axis):
        half = rows.shape[0] // 2
        rows = rows[:half].astype(f32) + swap(rows[half:].astype(kind), axis, bit).astype(f32)
    return rows


def pair_offsets(axis):
    offsets = [0]
    for bit in reversed(pair_bits(axis)):
        offsets = offsets + [offset ^ bit for offset in offsets]
    return offsets


def lookup(table, index):
    return sum(entry * (index == i).astype(jnp.int32) for i, entry in enumerate(table))


def ring_order(count):
    return list(range(0, count, 2)) + list(range(count - 1, 0, -2))


def ring_pairs(count, turn):
    order = ring_order(count)
    return [(order[r], order[(r + turn) % count]) for r in range(count)]


def ring_place(axis):
    count = lax.axis_size(axis)
    order = ring_order(count)
    place = [order.index(i) for i in range(count)]
    at = lookup(place, lax.axis_index(axis))
    return lambda ahead: lookup(order, (at + ahead + count) % count)


def together(*jobs):
    results = [None] * len(jobs)
    waiting = {}
    for i, job in enumerate(jobs):
        try:
            waiting[i] = next(job)
        except StopIteration as stop:
            results[i] = stop.value
    while waiting:
        waiting = lax.optimization_barrier(waiting)
        later = {}
        for i, received in waiting.items():
            try:
                later[i] = jobs[i].send(received)
            except StopIteration as stop:
                results[i] = stop.value
        waiting = later
    return results


def pair_gather_job(rows, axis):
    for bit in reversed(pair_bits(axis)):
        (other,) = yield (swap(rows, axis, bit),)
        rows = jnp.concatenate([rows, other], axis=0)
    return rows


def pair_scatter_job(rows, axis):
    for bit in pair_bits(axis):
        half = rows.shape[0] // 2
        (other,) = yield (swap(rows[half:].astype(bf16), axis, bit),)
        rows = rows[:half].astype(f32) + other.astype(f32)
    return rows


def ring_gather_job(block, axis, rows):
    count = lax.axis_size(axis)
    source = ring_place(axis)
    whole = jnp.zeros((count * rows, block.shape[1]), block.dtype)
    tails = jnp.zeros((count, 1, block.shape[1]), block.dtype)

    def put(whole, tails, got, ahead):
        at = source(ahead)
        return (
            lax.dynamic_update_slice_in_dim(whole, got[:rows], at * rows, 0),
            jnp.where(jnp.arange(count)[:, None, None] == at, got[rows : rows + 1][None], tails),
        )

    whole, tails = put(whole, tails, block, 0)
    one = two = block
    for k in range(1, count // 2 + 1):
        both = k < count - count // 2
        one = lax.ppermute(one, axis, ring_pairs(count, 1))
        if both:
            two = lax.ppermute(two, axis, ring_pairs(count, -1))
            one, two = yield (one, two)
            whole, tails = put(whole, tails, two, k)
        else:
            (one,) = yield (one,)
        whole, tails = put(whole, tails, one, -k)
    return whole, tails[:, 0]


def relative(values, axis):
    count = lax.axis_size(axis)
    wanted = jnp.asarray(pair_offsets(axis), jnp.int32) ^ lax.axis_index(axis)
    pick = wanted[:, None] == jnp.arange(count)[None]
    pick = pick.reshape(pick.shape + (1,) * (values.ndim - 1))
    return jnp.sum(jnp.where(pick, values[None], jnp.zeros((), values.dtype)), axis=1)


def absolute(values, axis):
    count = lax.axis_size(axis)
    wanted = jnp.asarray(pair_offsets(axis), jnp.int32) ^ lax.axis_index(axis)
    pick = jnp.arange(count)[:, None] == wanted[None]
    pick = pick.reshape(pick.shape + (1,) * (values.ndim - 1))
    return jnp.sum(jnp.where(pick, values[None], jnp.zeros((), values.dtype)), axis=1)


def ring_scatter_job(parts, axis):
    count = lax.axis_size(axis)
    source = ring_place(axis)
    part = lambda ahead: lax.dynamic_index_in_dim(parts, source(ahead), 0, keepdims=False)
    far = count // 2
    near = count - 1 - far
    one, two = part(far).astype(bf16), part(-near).astype(bf16)
    for k in range(far):
        one = lax.ppermute(one, axis, ring_pairs(count, 1))
        if k < near:
            two = lax.ppermute(two, axis, ring_pairs(count, -1))
        one, two = yield (one, two)
        if k < far - 1:
            one = (one.astype(f32) + part(far - k - 1)).astype(bf16)
        if k < near - 1:
            two = (two.astype(f32) + part(-(near - k - 1))).astype(bf16)
    return part(0) + one.astype(f32) + two.astype(f32)


def split_dot(a, b):
    a_hi, b_hi = a.astype(bf16), b.astype(bf16)
    a_lo = (a - a_hi.astype(f32)).astype(bf16)
    b_lo = (b - b_hi.astype(f32)).astype(bf16)
    dot = functools.partial(jnp.dot, preferred_element_type=f32)
    return dot(a_hi, b_hi) + (dot(a_hi, b_lo) + dot(a_lo, b_hi))


def chain_forward(m_ref, b_ref, s_ref):
    blocks, _, width = b_ref.shape

    def step(c, state):
        s_ref[c] = state
        return split_dot(m_ref[c], state) + b_ref[c]

    lax.fori_loop(0, blocks, step, jnp.zeros((DK, width), f32))


def chain_backward(mt_ref, d_ref, g_ref):
    blocks, _, width = d_ref.shape

    def step(i, grad):
        c = blocks - 1 - i
        g_ref[c] = grad
        return split_dot(mt_ref[c], grad) + d_ref[c]

    lax.fori_loop(0, blocks, step, jnp.zeros((DK, width), f32))


def run_chain(kernel, maps, terms):
    width = terms.shape[2]
    terms = jnp.pad(terms, ((0, 0), (0, 0), (0, -width % 128)))
    return pl.pallas_call(
        kernel,
        out_shape=jax.ShapeDtypeStruct(terms.shape, f32),
        in_specs=[pl.BlockSpec(memory_space=pltpu.VMEM)] * 2,
        out_specs=pl.BlockSpec(memory_space=pltpu.VMEM),
    )(maps, terms)[:, :, :width]


@jax.custom_vjp
def chain(maps, terms):
    return run_chain(chain_forward, maps, terms)


def chain_fwd(maps, terms):
    states = run_chain(chain_forward, maps, terms)
    return states, (maps, states)


def chain_bwd(saved, d_states):
    maps, states = saved
    grads = run_chain(chain_backward, jnp.swapaxes(maps, 1, 2), d_states)
    return jnp.einsum("ndv,nev->nde", grads, states, preferred_element_type=f32, precision=HIGH), grads


chain.defvjp(chain_fwd, chain_bwd)


def bdot(a, b, precision=HIGH):
    return jnp.einsum("nij,njk->nik", a, b, precision=precision, preferred_element_type=f32)


def inverse_of(strict_lower):
    size = strict_lower.shape[-1]
    rows_i = lax.broadcasted_iota(jnp.int32, (size, size), 0)
    cols_j = lax.broadcasted_iota(jnp.int32, (size, size), 1)
    inverse = jnp.broadcast_to(jnp.eye(size, dtype=f32), strict_lower.shape)
    width = 1
    while width < size:
        inside = (rows_i // (2 * width) == cols_j // (2 * width)) & (
            rows_i // width != cols_j // width
        )
        part = jnp.where(inside, strict_lower, 0.0)
        if width == 1:
            inverse = inverse - part
        else:
            inverse = inverse - bdot(bdot(inverse, part, HIGH), inverse, HIGH)
        width *= 2
    return inverse


@jax.custom_vjp
def unit_inverse(strict_lower):
    return inverse_of(strict_lower)


def unit_inverse_fwd(strict_lower):
    inverse = inverse_of(strict_lower)
    return inverse, inverse


def unit_inverse_bwd(inverse, d_inverse):
    flipped = jnp.swapaxes(inverse, 1, 2)
    return (-bdot(bdot(flipped, d_inverse, HIGH), flipped, HIGH),)


unit_inverse.defvjp(unit_inverse_fwd, unit_inverse_bwd)


def head_rule(queries, keys, values, betas, decays, seg_ids):
    length = queries.shape[0]
    size = min(BLOCK, length)
    blocks = length // size
    q = queries.reshape(blocks, size, DK)
    k = keys.reshape(blocks, size, DK)
    v = values.reshape(blocks, size, -1)
    beta = betas.reshape(blocks, size)
    seg = seg_ids.reshape(blocks, size)
    prev = jnp.concatenate([jnp.full((1,), -1, seg.dtype), seg[:-1, -1]])
    rows_i = lax.broadcasted_iota(jnp.int32, (size, size), 0)
    cols_j = lax.broadcasted_iota(jnp.int32, (size, size), 1)
    upto = (rows_i <= cols_j).astype(f32)
    gamma = jnp.dot(decays.reshape(blocks, size), upto, precision=HIGH)
    same = seg[:, :, None] == seg[:, None, :]
    incl = jnp.logical_and(same, (cols_j <= rows_i)[None])
    strict = jnp.logical_and(same, (cols_j < rows_i)[None]).astype(f32)
    diff = gamma[:, :, None] - gamma[:, None, :]
    lower = jnp.where(incl, jnp.exp(jnp.where(incl, diff, 0.0)), 0.0)
    carry_in = (seg == prev[:, None]).astype(f32)
    scaled = jnp.exp(gamma) * carry_in
    key_dots = jnp.einsum("nid,njd->nij", k, k, precision=HIGH)
    inverse = unit_inverse(beta[:, :, None] * lower * strict * key_dots)
    sides = jnp.concatenate([beta[:, :, None] * v, (beta * scaled)[:, :, None] * k], axis=2)
    fresh = bdot(inverse, sides, HIGH)
    new_v, new_k = fresh[:, :, : v.shape[2]], fresh[:, :, v.shape[2] :]
    scores = jnp.einsum("nid,njd->nij", q, k, precision=HIGH) * lower
    q_tilde = q * scaled[:, :, None] - bdot(scores, new_k)
    o_new = bdot(scores, new_v)
    tail = jnp.exp(gamma[:, -1:] - gamma) * (seg == seg[:, -1:]).astype(f32)
    key_tail = k * tail[:, :, None]
    keep = (jnp.exp(gamma[:, -1]) * carry_in[:, -1])[:, None, None]
    m_map = keep * jnp.eye(DK, dtype=f32)[None] - jnp.einsum("njd,nje->nde", key_tail, new_k, precision=HIGH)
    b_map = jnp.einsum("njd,njv->ndv", key_tail, new_v, precision=HIGH)
    states = chain(m_map, b_map)
    return (o_new + bdot(q_tilde, states)).reshape(length, -1)


def unit_core(proj, taps, proj_ab, a_log, dt_bias, same, seg_ids):
    extended = jnp.concatenate([jnp.zeros((CONV - 1, proj.shape[1]), f32), proj], axis=0)
    conv_out = convolve(extended, taps, same)
    queries = conv_out[:, :DK]
    keys = conv_out[:, DK : 2 * DK]
    values = conv_out[:, 2 * DK :]
    queries = (
        queries * lax.rsqrt(jnp.sum(queries * queries, axis=-1, keepdims=True) + EPS) * DK ** (-0.5)
    )
    keys = keys * lax.rsqrt(jnp.sum(keys * keys, axis=-1, keepdims=True) + EPS)
    betas = jax.nn.sigmoid(proj_ab[:, 0])
    decays = -jnp.exp(a_log) * jax.nn.softplus(proj_ab[:, 1] + dt_bias)
    return head_rule(queries, keys, values, betas, decays, seg_ids)


def out_gate(mixed, proj_og, gain, groups):
    squares = jnp.sum(mixed * mixed, axis=-1, keepdims=True)
    if groups is not None:
        squares = lax.psum(squares, "seq", axis_index_groups=groups)
    return mixed * lax.rsqrt(squares / DV + EPS) * gain * jax.nn.silu(proj_og)


class Heads:
    def __init__(self, w_qkv, w_og):
        self.ndp = lax.axis_size("dp")
        self.nseq = lax.axis_size("seq")
        self.split = self.nseq // HEADS
        self.wide = DV // self.split
        unit = lax.axis_index("seq")
        self.head = unit // self.split
        self.part = unit % self.split
        self.cq = w_qkv.shape[1]
        self.co = w_og.shape[1]
        self.direct = (
            self.split == 1
            and DK % self.cq == 0
            and (2 * DK + DV) == self.ndp * self.cq
            and DV == self.ndp * self.co
            and 2 * self.co == self.cq
        )
        if self.direct:
            per = DK // self.cq
            self.to_qkv, self.to_og = [], []
            for j in range(self.ndp * self.nseq):
                kind, head, place = 0, j // per, j % per
                if head >= HEADS:
                    kind, head = 1, head - HEADS
                if head >= HEADS:
                    own = j - 2 * HEADS * per
                    kind, head, place = 2, own // (DV // self.cq), own % (DV // self.cq)
                slot = kind * per + place
                self.to_qkv.append((j, slot * self.nseq + head))
                self.to_og.append((j, (j % self.ndp) * self.nseq + j // self.ndp))

    def back(self, pairs):
        return [(b, a) for a, b in pairs]

    def starts(self):
        base = 2 * HEADS * DK
        return (
            (self.head * DK, DK),
            ((HEADS + self.head) * DK, DK),
            (base + self.head * DV + self.part * self.wide, self.wide),
        )

    def fetch(self, w_qkv, conv_w, w_og):
        if not self.direct:
            full = lax.all_gather(w_qkv, BOTH, axis=1, tiled=True)
            taps = lax.all_gather(conv_w, BOTH, axis=1, tiled=True)
            gates = lax.all_gather(w_og, BOTH, axis=1, tiled=True)
            take = lambda a: jnp.concatenate(
                [lax.dynamic_slice_in_dim(a, s, n, 1) for s, n in self.starts()], axis=1
            )
            og = lax.dynamic_slice_in_dim(
                gates, self.head * DV + self.part * self.wide, self.wide, 1
            )
            return take(full), take(taps), og
        depth = w_qkv.shape[0]
        half = depth // 2
        padded = jnp.pad(conv_w, ((0, EDGE - CONV), (0, 0)))
        one = lax.ppermute(jnp.concatenate([w_qkv, padded], axis=0), BOTH, self.to_qkv)
        two = lax.ppermute(
            jnp.concatenate([w_og[:half], w_og[half:]], axis=1), BOTH, self.to_og
        )
        one, two = yield (one, two)
        mine = jnp.concatenate([one, two], axis=0)
        offsets = pair_offsets("dp")
        relative = yield from pair_gather_job(mine, "dp")
        relative = relative.reshape((self.ndp,) + mine.shape)
        places = [offsets.index(i) for i in range(self.ndp)]
        here = lax.axis_index("dp")
        all_slots = jnp.stack(
            [
                lax.dynamic_index_in_dim(relative, lookup(places, here ^ s), 0, keepdims=False)
                for s in range(self.ndp)
            ]
        )
        qkv = jnp.concatenate([all_slots[s, :depth] for s in range(self.ndp)], axis=1)
        taps = jnp.concatenate(
            [all_slots[s, depth : depth + CONV] for s in range(self.ndp)], axis=1
        )
        low = all_slots[:, depth + EDGE :]
        og = jnp.concatenate(
            [
                jnp.concatenate([low[s, :, : self.co], low[s, :, self.co :]], axis=0)
                for s in range(self.ndp)
            ],
            axis=1,
        )
        return qkv, taps, og

    def give(self, d_qkv, d_taps, d_og):
        depth = d_qkv.shape[0]
        half = depth // 2
        if not self.direct:
            outs = []
            for grad, total in ((d_qkv, 2 * HEADS * DK + HEADS * DV), (d_taps, None)):
                total = 2 * HEADS * DK + HEADS * DV
                full = jnp.zeros((grad.shape[0], total), f32)
                at = 0
                for start, n in self.starts():
                    full = lax.dynamic_update_slice_in_dim(
                        full, grad[:, at : at + n].astype(f32), start, 1
                    )
                    at += n
                outs.append(
                    lax.psum_scatter(full.astype(bf16), BOTH, scatter_dimension=1, tiled=True)
                )
            full = lax.dynamic_update_slice_in_dim(
                jnp.zeros((depth, HEADS * DV), f32),
                d_og.astype(f32),
                self.head * DV + self.part * self.wide,
                1,
            )
            og = lax.psum_scatter(full.astype(bf16), BOTH, scatter_dimension=1, tiled=True)
            return outs[0].astype(f32), outs[1].astype(f32), og.astype(f32)
        cq, co = self.cq, self.co
        taps = jnp.pad(d_taps.astype(bf16), ((0, EDGE - CONV), (0, 0)))
        blocks = jnp.stack(
            [
                jnp.concatenate(
                    [
                        d_qkv[:, s * cq : (s + 1) * cq],
                        taps[:, s * cq : (s + 1) * cq],
                        jnp.concatenate(
                            [
                                d_og[:half, s * co : (s + 1) * co],
                                d_og[half:, s * co : (s + 1) * co],
                            ],
                            axis=1,
                        ),
                    ],
                    axis=0,
                )
                for s in range(self.ndp)
            ]
        )
        here = lax.axis_index("dp")
        blocks = jnp.concatenate(
            [
                lax.dynamic_index_in_dim(blocks, here ^ offset, 0, keepdims=False)
                for offset in pair_offsets("dp")
            ],
            axis=0,
        )
        yield ()
        summed = (yield from pair_scatter_job(blocks, "dp")).astype(bf16)
        one = lax.ppermute(summed[: depth + EDGE], BOTH, self.back(self.to_qkv))
        two = lax.ppermute(summed[depth + EDGE :], BOTH, self.back(self.to_og))
        one, two = yield (one, two)
        one, two = one.astype(f32), two.astype(f32)
        return (
            one[:depth],
            one[depth : depth + CONV],
            jnp.concatenate([two[:, :co], two[:, co:]], axis=0),
        )


def halves_rounds(count):
    first, second = [], []
    for p in range(count):
        low = p < count // 2
        base = 2 * (p if low else p - count // 2)
        first.append((p, base if low else base + 1))
        second.append((p, base + 1 if low else base))
    return first, second


def local(
    block_input,
    segment_ids,
    norm_gain,
    w_qkv,
    w_ab,
    w_og,
    conv_w,
    a_log,
    dt_bias,
    o_gain,
    w_o,
    mlp_gain,
    w_gu,
    w_down,
    cotangent,
):
    heads = Heads(w_qkv, w_og)
    ndp, nseq, split, wide = heads.ndp, heads.nseq, heads.split, heads.wide
    rows = block_input[0]
    cot = cotangent[0]
    length, depth = rows.shape
    total = length * nseq
    small = norm_gain.shape[0]
    groups = None
    if split > 1:
        groups = [[h * split + i for i in range(split)] for h in range(HEADS)]

    full_o = lax.all_gather(w_o, BOTH, axis=0, tiled=True)
    half = w_gu.shape[1] // 2
    round_one, round_two = halves_rounds(ndp)
    low_half = lax.axis_index("dp") < ndp // 2
    even = lax.axis_index("dp") % 2 == 0

    def input_job():
        extra = jnp.concatenate(
            [norm_gain, mlp_gain, w_ab.reshape(-1), segment_ids[0].astype(bf16)]
        )
        used = extra.shape[0]
        extra = jnp.pad(extra, (0, EDGE * depth - used)).reshape(EDGE, depth)
        whole, tails = yield from ring_gather_job(
            jnp.concatenate([rows, extra], axis=0), "seq", length
        )
        params = yield from pair_gather_job(tails[None, :, : used - length], "dp")
        return whole, tails[:, used - length : used], absolute(params, "dp")

    def ffn_job():
        yield ()
        one = lax.ppermute(jnp.where(low_half, w_gu[:, :half], w_gu[:, half:]), "dp", round_one)
        two = lax.ppermute(jnp.where(low_half, w_gu[:, half:], w_gu[:, :half]), "dp", round_two)
        return (yield (one, two))

    (x_all, seg_ids, params), (unit_qkv, unit_taps, unit_og), (got_one, got_two) = together(
        input_job(), heads.fetch(w_qkv, conv_w, w_og), ffn_job()
    )
    seg_ids = seg_ids.astype(jnp.int32).reshape(total)
    gain_one = params[:, :, :small].reshape(-1).astype(f32)
    gain_two = params[:, :, small : 2 * small].reshape(-1).astype(f32)
    full_ab = params[:, :, 2 * small :].reshape(depth, 2 * HEADS)
    ffn = jnp.concatenate(
        [jnp.where(even, got_one, got_two), jnp.where(even, got_two, got_one), w_down.T], axis=1
    )
    ffn = lax.all_gather(ffn, "seq", axis=0, tiled=True)
    cot_late, _ = lax.optimization_barrier((cot, unit_og))
    cot_all = pair_gather(cot_late, "dp")
    full_gu, full_down_t = ffn[:, : 2 * half], ffn[:, 2 * half :]

    x_f = x_all.astype(f32)
    inv_one = lax.rsqrt(jnp.mean(x_f * x_f, axis=-1, keepdims=True) + EPS)
    normed = (x_f * inv_one * gain_one).astype(bf16)
    columns = jnp.concatenate([unit_qkv, unit_og], axis=1)
    projected = jnp.dot(normed, columns, preferred_element_type=f32)
    channels = 2 * DK + wide
    proj = projected[:, :channels].astype(bf16).astype(f32)
    proj_og = projected[:, channels:]
    pick = (
        jnp.arange(2 * HEADS)[:, None] == jnp.stack([heads.head, heads.head + HEADS])[None]
    ).astype(f32)
    unit_ab = jnp.dot(full_ab.astype(f32), pick).astype(bf16)
    proj_ab = jnp.dot(normed, unit_ab, preferred_element_type=f32)
    ext_ids = jnp.concatenate([jnp.full((CONV - 1,), -1, jnp.int32), seg_ids])
    same = jnp.stack([ext_ids[i : i + total] == seg_ids for i in range(CONV)], axis=1).astype(f32)
    at_head = jnp.arange(HEADS) == heads.head
    own_log = jnp.sum(jnp.where(at_head, a_log, 0.0))
    own_bias = jnp.sum(jnp.where(at_head, dt_bias, 0.0))
    mixed, core_back = jax.vjp(
        lambda *a: unit_core(*a, same, seg_ids),
        proj,
        unit_taps.astype(f32),
        proj_ab,
        own_log,
        own_bias,
    )
    own_gain = lax.dynamic_slice_in_dim(o_gain, heads.part * wide, wide)
    gated_f, gate_back = jax.vjp(
        lambda *a: out_gate(*a, groups), mixed, proj_og, own_gain
    )
    gated = gated_f.astype(bf16)
    gated_rows = exchange(gated.reshape(nseq, length, wide), "seq")
    gated_rows = jnp.swapaxes(gated_rows, 0, 1).reshape(length, nseq * wide)
    quarter = nseq * wide // ndp
    gated_all = []
    for offset in pair_offsets("dp"):
        piece = lax.dynamic_slice_in_dim(
            gated_rows, (lax.axis_index("dp") ^ offset) * quarter, quarter, 1
        )
        gated_all.append(piece if offset == 0 else swap(piece, "dp", offset))
    gated_all = jnp.concatenate(gated_all, axis=0)

    resid = rows.astype(f32) + jnp.dot(gated_rows, full_o, preferred_element_type=f32)
    normed2_f, rms2_back = jax.vjp(rms, resid, gain_two)
    normed2 = pair_gather(normed2_f.astype(bf16), "dp")
    joined = jnp.dot(normed2, full_gu, preferred_element_type=f32)
    act_f, act_back = jax.vjp(swiglu, joined[:, :half], joined[:, half:])
    act = act_f.astype(bf16)
    d_act = jnp.dot(cot_all, full_down_t, preferred_element_type=f32)
    d_gate, d_up = act_back(d_act)
    d_joined = jnp.concatenate([d_gate.astype(bf16), d_up.astype(bf16)], axis=1)
    d_normed2 = pair_scatter(
        jnp.einsum("lf,df->ld", d_joined, full_gu, preferred_element_type=f32), "dp", f32
    )
    d_resid_n, grad_g2 = rms2_back(d_normed2)
    d_resid = cot.astype(f32) + d_resid_n
    d_resid_b = d_resid.astype(bf16)
    out_part = jnp.einsum("lf,df->ld", act, full_down_t, preferred_element_type=f32)
    out = (resid + pair_scatter(out_part, "dp")).astype(bf16)
    grad_o = jnp.einsum(
        "lv,ld->vd", gated_all, pair_gather(d_resid_b, "dp"), preferred_element_type=f32
    ).reshape(nseq, quarter // nseq, depth)
    pieces = depth // quarter
    grad_o = jnp.concatenate(
        [grad_o[:, :, i * quarter : (i + 1) * quarter] for i in range(pieces)], axis=1
    )
    grad_ffn = jnp.concatenate(
        [
            jnp.einsum("ld,lf->df", normed2, d_joined, preferred_element_type=f32),
            jnp.einsum("ld,lf->df", cot_all, act, preferred_element_type=f32),
            grad_o.reshape(depth, quarter),
        ],
        axis=1,
    ).astype(bf16)
    grad_ffn = lax.psum_scatter(grad_ffn, "seq", scatter_dimension=0, tiled=True)
    grad_down = grad_ffn[:, 2 * half : 3 * half].T.astype(f32)
    grad_o = grad_ffn[:, 3 * half :].astype(f32).reshape(pieces, quarter // nseq, quarter)
    grad_o = jnp.swapaxes(grad_o, 0, 1).reshape(quarter // nseq, depth)
    g_gate, g_up = grad_ffn[:, :half], grad_ffn[:, half : 2 * half]

    d_gated_rows = jnp.einsum("ld,vd->lv", d_resid_b, full_o, preferred_element_type=f32)
    d_gated_rows = jnp.swapaxes(d_gated_rows.reshape(length, nseq, wide), 0, 1)
    d_gated = exchange(d_gated_rows, "seq").reshape(total, wide)
    d_mixed, d_og, grad_ogain = gate_back(d_gated)
    d_proj, d_taps, d_ab, d_log, d_bias = core_back(d_mixed)
    d_columns = jnp.concatenate([d_proj.astype(bf16), d_og.astype(bf16)], axis=1)
    d_ab_b = d_ab.astype(bf16)
    d_normed_part = jnp.einsum(
        "lc,dc->ld", d_columns, columns, preferred_element_type=f32
    ) + jnp.einsum("lc,dc->ld", d_ab_b, unit_ab, preferred_element_type=f32)
    grad_g1 = jnp.sum(d_normed_part * (x_f * inv_one), axis=0)
    grad_columns = jnp.einsum(
        "ld,lc->dc", normed, d_columns, preferred_element_type=f32
    ).astype(bf16)
    grad_ab = jnp.einsum("ld,lc->dc", normed, d_ab_b, preferred_element_type=f32)
    grad_ab = jnp.dot(grad_ab, pick.T, precision=HIGH)
    owned = jnp.concatenate(
        [
            grad_g1.reshape(ndp, nseq, small),
            grad_g2.reshape(ndp, nseq, small),
            grad_ab.reshape(ndp, nseq, small * 2 * HEADS),
        ],
        axis=2,
    )
    owned = jnp.swapaxes(relative(owned, "dp"), 0, 1)
    owned = relative(owned, "seq")
    shared = jnp.concatenate(
        [
            jnp.where(at_head, d_log, 0.0),
            jnp.where(at_head, d_bias, 0.0),
            lax.dynamic_update_slice_in_dim(
                jnp.zeros((DV,), f32), grad_ogain, heads.part * wide, 0
            ),
        ]
    )
    count = shared.shape[0]

    def shared_job():
        mine, everyones = owned, shared
        for axis in ("seq", "dp"):
            for bit in pair_bits(axis):
                half = mine.shape[0] // 2
                sent = jnp.concatenate([mine[half:].reshape(-1), everyones])
                (got,) = yield (swap(sent, axis, bit),)
                mine = mine[:half] + got[:-count].reshape(mine[:half].shape)
                everyones = everyones + got[-count:]
            mine = mine[0]
        return jnp.concatenate([mine, everyones])

    def ffn_back_job():
        for _ in range(3):
            yield ()
        one, two = jnp.where(even, g_gate, g_up), jnp.where(even, g_up, g_gate)
        return (
            yield (
                lax.ppermute(one, "dp", heads.back(round_one)),
                lax.ppermute(two, "dp", heads.back(round_two)),
            )
        )

    d_normed, (grad_qkv, grad_conv, grad_og), owned, (back_one, back_two) = together(
        ring_scatter_job(d_normed_part.reshape(nseq, length, depth), "seq"),
        heads.give(grad_columns[:, :channels], d_taps, grad_columns[:, channels:]),
        shared_job(),
        ffn_back_job(),
    )
    grad_gu = jnp.where(
        low_half,
        jnp.concatenate([back_one, back_two], axis=1),
        jnp.concatenate([back_two, back_one], axis=1),
    ).astype(f32)
    _, rms1_back = jax.vjp(lambda r: rms(r, gain_one), rows.astype(f32))
    (d_rows_n,) = rms1_back(d_normed)
    d_rows = (d_resid + d_rows_n).astype(bf16)
    return (
        out[None],
        d_rows[None],
        owned[:small],
        grad_qkv,
        owned[2 * small : -count].reshape(small, 2 * HEADS),
        grad_og,
        grad_conv,
        owned[-count:][:HEADS],
        owned[-count:][HEADS : 2 * HEADS],
        owned[-count:][2 * HEADS :],
        grad_o,
        owned[small : 2 * small],
        grad_gu,
        grad_down,
    )


def solution(mesh):
    return jax.shard_map(
        local,
        mesh=mesh,
        in_specs=(
            P("dp", "seq", None),
            P("dp", "seq"),
            P(("dp", "seq")),
            P(None, ("dp", "seq")),
            P(("dp", "seq"), None),
            P(None, ("dp", "seq")),
            P(None, ("dp", "seq")),
            P(),
            P(),
            P(),
            P(("dp", "seq"), None),
            P(("dp", "seq")),
            P("seq", "dp"),
            P("dp", "seq"),
            P("dp", "seq", None),
        ),
        out_specs=(
            P("dp", "seq", None),
            P("dp", "seq", None),
            P(("dp", "seq")),
            P(None, ("dp", "seq")),
            P(("dp", "seq"), None),
            P(None, ("dp", "seq")),
            P(None, ("dp", "seq")),
            P(),
            P(),
            P(),
            P(("dp", "seq"), None),
            P(("dp", "seq")),
            P("seq", "dp"),
            P("dp", "seq"),
        ),
        check_vma=False,
    )
```
